256 devices in a mesh: blk: 32 (over z_lo, y, core), shard: 8 (over x, z_hi).
Axes of the slice: x: 4, y: 4, z: 8 (z_hi: 2, z_lo: 4; z = z_hi * 4 + z_lo), core: 2. Of those that a mesh axis runs over, the one named last changes fastest.
Arguments:
- user_factors: float32 [262144, 128], P(('blk', 'shard')), may hold values from -2 to 2
- item_factors: float32 [16384, 128], P(('blk', 'shard')), may hold values from -2 to 2
- ratings: bfloat16 [2, 262144, 512], P(None, ('blk', 'shard')), may hold values from -6 to 6
- observed: int32 [2, 262144, 512], P(None, ('blk', 'shard')), may hold values 0 or 1
- plan: int32 [2], replicated, may hold values from 1 to 31
- user_noise: float32 [2, 262144, 128], P(None, ('blk', 'shard')), may hold values from -1 to 1
- item_noise: float32 [2, 16384, 128], P(None, 'blk'), may hold values from -1 to 1
Outputs:
- users_out: float32 [262144, 128], P(('blk', 'shard'))
- items_out: float32 [16384, 128], P(('blk', 'shard'))
The draws below stay inside these ranges and needn't reach their ends.
Inputs may be any that keep to these rules, and one draw needn't show every extreme that they name: `plan`: each entry is a number of cycle steps between 1 and 31.
All inputs are finite; a program needn't handle non-finite values. No bound on the sum of `observed` on one device may be relied on, other than what follows from the above.
Results may differ from the reference program's by a relative error of at most 0.0048.
Values may be sent and summed in bfloat16 or wider, within the bound.
No kernel may reach another device: no remote copies, remote signals or barrier semaphores. Data moves between devices by JAX's collectives and lax.ppermute only.
A program may use at most 64 MiB of HBM per device.

```python
import jax
import jax.numpy as jnp
from jax import lax

K = 128
ITEMS = 16384
USR_DEV = 1024
STRATA = 2
ITEM_BLK = 512
USERS = 262144
N_BLK = 32
N_SHARD = 8


def touch_ends(array, key, least, top_value):
    index_at = [jax.random.randint(jax.random.fold_in(key, axis), (), 0, length) for axis, length in enumerate(array.shape)]
    longest = array.shape.index(max(array.shape))
    neighbour = index_at[:longest] + [(index_at[longest] + 1) % array.shape[longest]] + index_at[longest + 1:]
    return array.at[tuple(index_at)].set(least).at[tuple(neighbour)].set(top_value)


def block_scale(key, shape, shards, least, high):
    def one(axis_at, blocks):
        steps = jax.random.uniform(jax.random.fold_in(jax.random.fold_in(key, 6), axis_at), (blocks,), jnp.float32, least / len(shards), high / len(shards))
        return jnp.repeat(jnp.exp(steps), shape[axis_at] // blocks).reshape((-1,) + (1,) * (len(shape) - axis_at - 1))

    loudness = one(*shards[0])
    for cut in shards[1:]:
        loudness = loudness * one(*cut)
    return loudness


def normal_values(own_key, dims, width, reach, pieces=(), held_as=jnp.bfloat16):
    drawn = width * jax.random.normal(own_key, dims, jnp.float32)
    if pieces:
        drawn = drawn * block_scale(own_key, dims, pieces, -0.22, 0.18)
    return jnp.clip(drawn, -reach, reach).astype(held_as)


def setup_inputs(seed: int = 0) -> dict:
    streams_of = jax.random.split(jax.random.key(seed), 8)
    user_factors = normal_values(streams_of[0], (USERS, K), 0.3, 2.0, ((0, 256),), jnp.float32)
    item_factors = normal_values(streams_of[1], (ITEMS, K), 0.3, 2.0, ((0, 256),), jnp.float32)
    ratings = normal_values(streams_of[2], (STRATA, USERS, ITEM_BLK), 1.0, 6.0, ((1, 256),))
    observed = touch_ends((jax.random.randint(streams_of[3], (STRATA, USERS, ITEM_BLK), 0, 2) < 1).astype(jnp.int32), jax.random.fold_in(streams_of[3], 1), 0, 1)
    plan = jax.random.randint(streams_of[4], (STRATA,), 1, N_BLK).astype(jnp.int32)
    user_noise = normal_values(streams_of[5], (STRATA, USERS, K), 0.15, 1.0, ((1, 256),), jnp.float32)
    item_noise = normal_values(streams_of[6], (STRATA, ITEMS, K), 0.15, 1.0, ((1, 32),), jnp.float32)
    return {"user_factors": user_factors, "item_factors": item_factors, "ratings": ratings, "observed": observed, "plan": plan, "user_noise": user_noise, "item_noise": item_noise}


user_scale = 12.0
item_scale = 30.0
prior = 1.0


def reference(user_factors, item_factors, ratings, observed, plan, user_noise, item_noise):
    user_rate = user_scale / ITEM_BLK
    item_rate = item_scale / (N_SHARD * USR_DEV)
    users_now = user_factors.reshape(N_BLK, N_SHARD * USR_DEV, K)
    items_now = item_factors.reshape(N_BLK, ITEM_BLK, K)
    offset = jnp.zeros((), jnp.int32)
    cycle = jnp.arange(N_BLK, dtype=jnp.int32)

    def one_position(packed):
        users_pos, rating_tile, observed_tile, items_pos, noise_users, noise_items = packed
        users_half = users_pos.astype(jnp.bfloat16)
        items_half = items_pos.astype(jnp.bfloat16)
        predicted = jnp.dot(users_half, items_half.T, preferred_element_type=jnp.float32)
        errors = (observed_tile.astype(jnp.float32) * (rating_tile.astype(jnp.float32) - predicted)).astype(jnp.bfloat16)
        user_grad = jnp.dot(errors, items_half, preferred_element_type=jnp.float32)
        item_grad = lax.dot_general(errors, users_half, (((0,), (0,)), ((), ())), preferred_element_type=jnp.float32)
        users_new = users_pos + user_rate * (user_grad - prior * users_pos) + noise_users
        items_new = items_pos + item_rate * (item_grad - prior * items_pos) + noise_items
        return users_new, items_new

    for stratum in range(STRATA):
        offset = (offset + plan[stratum]) % N_BLK
        met = ((cycle - offset) % N_BLK).astype(jnp.int32)
        items_cycle = jnp.take(items_now, met, axis=0)
        users_now, items_cycle = lax.map(one_position, (
            users_now,
            ratings[stratum].reshape(N_BLK, N_SHARD * USR_DEV, ITEM_BLK),
            observed[stratum].reshape(N_BLK, N_SHARD * USR_DEV, ITEM_BLK),
            items_cycle,
            user_noise[stratum].reshape(N_BLK, N_SHARD * USR_DEV, K),
            item_noise[stratum].reshape(N_BLK, ITEM_BLK, K)))
        home = ((cycle + offset) % N_BLK).astype(jnp.int32)
        items_now = jnp.take(items_cycle, home, axis=0)
    return users_now.reshape(USERS, K), items_now.reshape(ITEMS, K)
```

```python
import jax
import jax.numpy as jnp
from jax import lax
from jax.experimental import pallas as pl
from jax.experimental.pallas import tpu as pltpu
from jax.sharding import PartitionSpec as P


user_scale = 12.0
item_scale = 30.0
prior = 1.0

FLAT = ("blk", "shard")
TWINS = 2
CHUNK = 256


def pairs(blk, shard, distance, x_step, flip):
    ring = shard // TWINS
    out = []
    for b in range(blk):
        for s in range(shard):
            x, twin = s // TWINS, s % TWINS
            to = ((x + x_step) % ring) * TWINS + (twin + flip) % TWINS
            out.append((b * shard + s, ((b + distance) % blk) * shard + to))
    return out


def rotated_sum(share, steps):
    blk, shard = lax.axis_size("blk"), lax.axis_size("shard")

    def branch(distance):
        def move(value):
            own = value
            if distance:
                own = lax.ppermute(value, FLAT, pairs(blk, shard, distance, 0, 0))
            return own + lax.ppermute(value, FLAT, pairs(blk, shard, distance, 0, 1))

        return move

    return lax.switch(steps, [branch(d) for d in range(blk)], share)


def moved_along_x(value, x_step):
    blk, shard = lax.axis_size("blk"), lax.axis_size("shard")
    return lax.ppermute(value, FLAT, pairs(blk, shard, 0, x_step, 0))


def stratum_kernel(ring, user_rate, at_ref, *refs):
    pieces, refs = refs[:ring], refs[ring:]
    users_ref, ratings_ref, observed_ref, noise_ref = refs[:4]
    users_out_ref, grads, (items_ref, sum_ref) = refs[4], refs[5 : 5 + ring], refs[5 + ring :]
    step = pl.program_id(0)
    rows = pieces[0].shape[0]
    x = at_ref[1]

    @pl.when(step == 0)
    def _():
        for k in range(ring):
            place = lax.rem(x + ring - k, ring) * rows
            items_ref[pl.ds(pl.multiple_of(place, rows), rows), :] = pieces[k][...]
        sum_ref[...] = jnp.zeros_like(sum_ref)

    items = items_ref[...]
    users = users_ref[...]
    users_half = users.astype(jnp.bfloat16)
    predicted = lax.dot_general(
        users_half, items, (((1,), (1,)), ((), ())), preferred_element_type=jnp.float32
    )
    errors = (
        observed_ref[0].astype(jnp.float32) * (ratings_ref[0].astype(jnp.float32) - predicted)
    ).astype(jnp.bfloat16)
    sum_ref[...] += lax.dot_general(
        errors, users_half, (((0,), (0,)), ((), ())), preferred_element_type=jnp.float32
    )
    user_grad = jnp.dot(errors, items, preferred_element_type=jnp.float32)
    users_out_ref[...] = users + user_rate * (user_grad - prior * users) + noise_ref[0]

    @pl.when(step == pl.num_programs(0) - 1)
    def _():
        for k in range(ring):
            place = lax.rem(x + k, ring) * rows
            grads[k][...] = sum_ref[pl.ds(pl.multiple_of(place, rows), rows), :]


def stratum(at, pieces, users, ratings, observed, noise, user_rate):
    ring = len(pieces)
    rows, rank = pieces[0].shape
    user_rows = users.shape[0]
    items = ratings.shape[2]
    whole = pl.BlockSpec((rows, rank), lambda i, at: (0, 0))
    chunk = pl.BlockSpec((CHUNK, rank), lambda i, at: (i, 0))
    tile = pl.BlockSpec((1, CHUNK, items), lambda i, at: (at[0], i, 0))
    noise_chunk = pl.BlockSpec((1, CHUNK, rank), lambda i, at: (at[0], i, 0))

    def body(*refs):
        stratum_kernel(ring, user_rate, *refs)

    out = pl.pallas_call(
        body,
        out_shape=[jax.ShapeDtypeStruct(users.shape, jnp.float32)]
        + [jax.ShapeDtypeStruct((rows, rank), jnp.float32)] * ring,
        grid_spec=pltpu.PrefetchScalarGridSpec(
            num_scalar_prefetch=1,
            grid=(user_rows // CHUNK,),
            in_specs=[whole] * ring + [chunk, tile, tile, noise_chunk],
            out_specs=[chunk] + [whole] * ring,
            scratch_shapes=[
                pltpu.VMEM((items, rank), jnp.bfloat16),
                pltpu.VMEM((items, rank), jnp.float32),
            ],
        ),
        input_output_aliases={1 + ring: 0},
        name="stratum",
    )(at, *pieces, users, ratings, observed, noise)
    return out[0], out[1:]


def local(user_factors, item_factors, ratings, observed, plan, user_noise, item_noise):
    blk, shard = lax.axis_size("blk"), lax.axis_size("shard")
    ring = shard // TWINS
    user_rows = user_factors.shape[0]
    piece_rows = item_factors.shape[0]
    rows = piece_rows * TWINS
    user_rate = user_scale / ratings.shape[2]
    item_rate = item_scale / (shard * user_rows)
    strata = ratings.shape[0]
    x = lax.axis_index("shard") // TWINS
    twin = lax.axis_index("shard") % TWINS

    steps = jnp.concatenate([plan, (-jnp.sum(plan))[None]]) % blk
    zeros = jnp.zeros_like(item_factors)
    share = jnp.where(
        twin == 0,
        jnp.concatenate([item_factors, zeros], 0),
        jnp.concatenate([zeros, item_factors], 0),
    )

    def one(t, users, items):
        half = items.astype(jnp.bfloat16)
        pieces = [half] + [moved_along_x(half, k) for k in range(1, ring)]
        users, grads = stratum(
            jnp.stack([t, x]).astype(jnp.int32), pieces, users, ratings, observed, user_noise, user_rate
        )
        grad = grads[0]
        for k in range(1, ring):
            grad = grad + moved_along_x(grads[k], k)
        noise = lax.dynamic_slice(item_noise, (t, x * rows, 0), (1, rows, item_noise.shape[2]))[0]
        kept = jnp.where(twin == 0, items - item_rate * prior * items + noise, 0.0)
        return users, kept + item_rate * grad

    def trip(t, carry):
        users, share = carry
        items = rotated_sum(share, lax.dynamic_index_in_dim(steps, t, keepdims=False))
        return lax.cond(t < strata, one, lambda t, users, items: (users, items), t, users, items)

    users, items = lax.fori_loop(0, strata + 1, trip, (user_factors, share))
    piece = lax.dynamic_slice_in_dim(items, twin * piece_rows, piece_rows, 0)
    return users, piece


def solution(mesh):
    in_specs = (
        P(("blk", "shard"), None),
        P(("blk", "shard"), None),
        P(None, ("blk", "shard"), None),
        P(None, ("blk", "shard"), None),
        P(),
        P(None, ("blk", "shard"), None),
        P(None, "blk", None),
    )
    out_specs = (P(("blk", "shard"), None), P(("blk", "shard"), None))
    return jax.shard_map(local, mesh=mesh, in_specs=in_specs, out_specs=out_specs, check_vma=False)
```

```python
import jax
import jax.numpy as jnp
from jax import lax
from jax.experimental import pallas as pl
from jax.experimental.pallas import tpu as pltpu
from jax.sharding import PartitionSpec as P


user_scale = 12.0
item_scale = 30.0
prior = 1.0

FLAT = ("blk", "shard")
TWINS = 2
LOW = 8
CHUNK = 256


def pairs(blk, shard, distance, x_step):
    ring = shard // TWINS
    out = []
    for b in range(blk):
        for s in range(shard):
            x, twin = s // TWINS, s % TWINS
            far = (twin * blk + b + distance) % (TWINS * blk)
            to = ((x + x_step) % ring) * TWINS + far // blk
            out.append((b * shard + s, (far % blk) * shard + to))
    return out


def moved(value, distance, x_step=0):
    blk, shard = lax.axis_size("blk"), lax.axis_size("shard")
    if distance % (TWINS * blk) == 0 and x_step == 0:
        return value
    return lax.ppermute(value, FLAT, pairs(blk, shard, distance, x_step))


def rotated_sum(share, steps):
    blk = lax.axis_size("blk")
    low = (steps + LOW // 2) % LOW
    high = ((steps - (low - LOW // 2)) % blk) // LOW

    def first(d):
        return lambda v: moved(v, d)

    def second(d):
        return lambda v: moved(v, d) + moved(v, d + blk)

    share = lax.switch(low, [first(d - LOW // 2) for d in range(LOW)], share)
    return lax.switch(high, [second(d * LOW) for d in range(blk // LOW)], share)


def errors_kernel(ring, at_ref, *refs):
    pieces, refs = refs[:ring], refs[ring:]
    users_ref, ratings_ref, observed_ref, errors_ref = refs[:4]
    grads, items_ref, sum_ref = refs[4 : 4 + ring], refs[4 + ring], refs[5 + ring]
    step = pl.program_id(0)
    rows = pieces[0].shape[0]
    x = at_ref[1]

    @pl.when(step == 0)
    def _():
        for k in range(ring):
            place = lax.rem(x + ring - k, ring) * rows
            items_ref[pl.ds(pl.multiple_of(place, rows), rows), :] = pieces[k][...]
        sum_ref[...] = jnp.zeros_like(sum_ref)

    users_half = users_ref[...].astype(jnp.bfloat16)
    predicted = lax.dot_general(
        users_half, items_ref[...], (((1,), (1,)), ((), ())), preferred_element_type=jnp.float32
    )
    errors = (
        observed_ref[0].astype(jnp.float32) * (ratings_ref[0].astype(jnp.float32) - predicted)
    ).astype(jnp.bfloat16)
    errors_ref[...] = errors
    sum_ref[...] += lax.dot_general(
        users_half, errors, (((0,), (0,)), ((), ())), preferred_element_type=jnp.float32
    )

    @pl.when(step == pl.num_programs(0) - 1)
    def _():
        for k in range(ring):
            place = lax.rem(x + k, ring) * rows
            grads[k][...] = sum_ref[:, pl.ds(pl.multiple_of(place, rows), rows)].T


def users_kernel(user_rate, at_ref, items_ref, errors_ref, users_ref, noise_ref, out_ref):
    users = users_ref[...]
    grad = jnp.dot(errors_ref[...], items_ref[...], preferred_element_type=jnp.float32)
    out_ref[...] = users + user_rate * (grad - prior * users) + noise_ref[0]


def stratum_errors(at, pieces, users, ratings, observed):
    ring = len(pieces)
    rows, rank = pieces[0].shape
    user_rows = users.shape[0]
    items = ratings.shape[2]
    whole = pl.BlockSpec((rows, rank), lambda i, at: (0, 0))
    chunk = pl.BlockSpec((CHUNK, rank), lambda i, at: (i, 0))
    tile = pl.BlockSpec((1, CHUNK, items), lambda i, at: (at[0], i, 0))

    def body(*refs):
        errors_kernel(ring, *refs)

    out = pl.pallas_call(
        body,
        out_shape=[jax.ShapeDtypeStruct((user_rows, items), jnp.bfloat16)]
        + [jax.ShapeDtypeStruct((rows, rank), jnp.float32)] * ring
        + [jax.ShapeDtypeStruct((items, rank), jnp.bfloat16)],
        grid_spec=pltpu.PrefetchScalarGridSpec(
            num_scalar_prefetch=1,
            grid=(user_rows // CHUNK,),
            in_specs=[whole] * ring + [chunk, tile, tile],
            out_specs=[pl.BlockSpec((CHUNK, items), lambda i, at: (i, 0))]
            + [whole] * ring
            + [pl.BlockSpec((items, rank), lambda i, at: (0, 0))],
            scratch_shapes=[pltpu.VMEM((rank, items), jnp.float32)],
        ),
        name="errors",
    )(at, *pieces, users, ratings, observed)
    return out[0], out[1 : 1 + ring], out[1 + ring]


def users_update(at, items, errors, users, noise, user_rate):
    user_rows, rank = users.shape
    chunk = pl.BlockSpec((CHUNK, rank), lambda i, at: (i, 0))

    def body(*refs):
        users_kernel(user_rate, *refs)

    return pl.pallas_call(
        body,
        out_shape=jax.ShapeDtypeStruct(users.shape, jnp.float32),
        grid_spec=pltpu.PrefetchScalarGridSpec(
            num_scalar_prefetch=1,
            grid=(user_rows // CHUNK,),
            in_specs=[
                pl.BlockSpec(items.shape, lambda i, at: (0, 0)),
                pl.BlockSpec((CHUNK, items.shape[0]), lambda i, at: (i, 0)),
                chunk,
                pl.BlockSpec((1, CHUNK, rank), lambda i, at: (at[0], i, 0)),
            ],
            out_specs=chunk,
        ),
        input_output_aliases={3: 0},
        name="users",
    )(at, items, errors, users, noise)


def local(user_factors, item_factors, ratings, observed, plan, user_noise, item_noise):
    blk, shard = lax.axis_size("blk"), lax.axis_size("shard")
    ring = shard // TWINS
    user_rows = user_factors.shape[0]
    piece_rows = item_factors.shape[0]
    rows = piece_rows * TWINS
    user_rate = user_scale / ratings.shape[2]
    item_rate = item_scale / (shard * user_rows)
    strata = ratings.shape[0]
    x = lax.axis_index("shard") // TWINS
    twin = lax.axis_index("shard") % TWINS

    steps = [plan[t] for t in range(strata)]
    steps.append((-sum(steps)) % blk)
    zeros = jnp.zeros_like(item_factors)
    share = jnp.where(
        twin == 0,
        jnp.concatenate([item_factors, zeros], 0),
        jnp.concatenate([zeros, item_factors], 0),
    )

    def one(t, users, items):
        half = items.astype(jnp.bfloat16)
        pieces = [half] + [moved(half, 0, k) for k in range(1, ring)]
        at = jnp.stack([t, x]).astype(jnp.int32)
        errors, grads, gathered = stratum_errors(at, pieces, users, ratings, observed)
        arrived = [grads[0]] + [moved(grads[k], 0, k) for k in range(1, ring)]
        users = users_update(at, gathered, errors, users, user_noise, user_rate)
        noise = lax.dynamic_slice(item_noise, (t, x * rows, 0), (1, rows, item_noise.shape[2]))[0]
        kept = jnp.where(twin == 0, items - item_rate * prior * items + noise, 0.0)
        return users, kept + item_rate * sum(arrived[1:], arrived[0])

    def trip(t, carry):
        users, share = carry
        step = steps[strata]
        for k in range(strata):
            step = jnp.where(t == k, steps[k], step)
        items = rotated_sum(share, step)
        return lax.cond(t < strata, one, lambda t, users, items: (users, items), t, users, items)

    users, items = lax.fori_loop(0, strata + 1, trip, (user_factors, share))
    piece = lax.dynamic_slice_in_dim(items, twin * piece_rows, piece_rows, 0)
    return users, piece


def solution(mesh):
    in_specs = (
        P(("blk", "shard"), None),
        P(("blk", "shard"), None),
        P(None, ("blk", "shard"), None),
        P(None, ("blk", "shard"), None),
        P(),
        P(None, ("blk", "shard"), None),
        P(None, "blk", None),
    )
    out_specs = (P(("blk", "shard"), None), P(("blk", "shard"), None))
    return jax.shard_map(local, mesh=mesh, in_specs=in_specs, out_specs=out_specs, check_vma=False)
```

```python
import jax
import jax.numpy as jnp
from jax import lax
from jax.experimental import pallas as pl
from jax.experimental.pallas import tpu as pltpu
from jax.sharding import PartitionSpec as P


user_scale = 12.0
item_scale = 30.0
prior = 1.0

FLAT = ("blk", "shard")
TWINS = 2
LOW = 8
CHUNK = 256
UNSEEN = 2.0**20


def pairs(blk, shard, distance, x_step):
    ring = shard // TWINS
    out = []
    for b in range(blk):
        for s in range(shard):
            x, twin = s // TWINS, s % TWINS
            far = (twin * blk + b + distance) % (TWINS * blk)
            to = ((x + x_step) % ring) * TWINS + far // blk
            out.append((b * shard + s, (far % blk) * shard + to))
    return out


def moved(value, distance, x_step=0):
    blk, shard = lax.axis_size("blk"), lax.axis_size("shard")
    if distance % (TWINS * blk) == 0 and x_step == 0:
        return value
    return lax.ppermute(value, FLAT, pairs(blk, shard, distance, x_step))


def rotated_sum(share, steps):
    blk = lax.axis_size("blk")
    low = (steps + LOW // 2) % LOW
    high = ((steps - (low - LOW // 2)) % blk) // LOW

    def first(d):
        return lambda v: moved(v, d)

    def second(d):
        return lambda v: lax.optimization_barrier(moved(v, d) + moved(v, d + blk))

    share = lax.switch(low, [first(d - LOW // 2) for d in range(LOW)], share)
    return lax.switch(high, [second(d * LOW) for d in range(blk // LOW)], share)


def prepare_kernel(at_ref, observed_ref, ratings_ref, start_ref, held_ref, coded_ref, users_ref):
    step = pl.program_id(0)
    rows = pl.ds(pl.multiple_of(step * CHUNK, CHUNK), CHUNK)
    ratings = ratings_ref[0].astype(jnp.float32)
    coded_ref[rows, :] = jnp.where(observed_ref[0] != 0, ratings, UNSEEN).astype(jnp.bfloat16)

    @pl.when(at_ref[0] == 0)
    def _():
        users_ref[rows, :] = start_ref[...]

    @pl.when(at_ref[0] != 0)
    def _():
        users_ref[rows, :] = held_ref[rows, :]


def errors_kernel(ring, at_ref, *refs):
    pieces, refs = refs[:ring], refs[ring:]
    users_ref, coded_ref, errors_ref = refs[:3]
    grads, items_ref, sum_ref = refs[3 : 3 + ring], refs[3 + ring], refs[4 + ring]
    rows = pieces[0].shape[0]
    x = at_ref[1]
    for k in range(ring):
        place = lax.rem(x + ring - k, ring) * rows
        items_ref[pl.ds(pl.multiple_of(place, rows), rows), :] = pieces[k][...]
    items = items_ref[...]
    total = None
    for c in range(users_ref.shape[0] // CHUNK):
        at = pl.ds(c * CHUNK, CHUNK)
        users_half = users_ref[at, :].astype(jnp.bfloat16)
        predicted = lax.dot_general(
            users_half, items, (((1,), (1,)), ((), ())), preferred_element_type=jnp.float32
        )
        coded = coded_ref[at, :].astype(jnp.float32)
        errors = jnp.where(coded < 0.5 * UNSEEN, coded - predicted, 0.0).astype(jnp.bfloat16)
        errors_ref[at, :] = errors
        part = lax.dot_general(
            users_half, errors, (((0,), (0,)), ((), ())), preferred_element_type=jnp.float32
        )
        total = part if total is None else total + part
    sum_ref[...] = total
    for k in range(ring):
        place = lax.rem(x + k, ring) * rows
        grads[k][...] = sum_ref[:, pl.ds(pl.multiple_of(place, rows), rows)].T


def users_kernel(user_rate, items_ref, errors_ref, users_ref, noise_ref, out_ref):
    items = items_ref[...]
    for c in range(users_ref.shape[0] // CHUNK):
        at = pl.ds(c * CHUNK, CHUNK)
        users = users_ref[at, :]
        grad = jnp.dot(errors_ref[at, :], items, preferred_element_type=jnp.float32)
        out_ref[at, :] = users + user_rate * (grad - prior * users) + noise_ref[at, :]


SMALL = pltpu.CompilerParams(vmem_limit_bytes=12 * 2**20)
IN_VMEM = pl.BlockSpec(memory_space=pltpu.VMEM)


def prepare(at, observed, ratings, start, held):
    user_rows, rank = start.shape
    items = ratings.shape[2]
    tile = pl.BlockSpec((1, CHUNK, items), lambda i, at: (at[0], i, 0))
    return pl.pallas_call(
        prepare_kernel,
        out_shape=[
            jax.ShapeDtypeStruct((user_rows, items), jnp.bfloat16),
            jax.ShapeDtypeStruct((user_rows, rank), jnp.float32),
        ],
        grid_spec=pltpu.PrefetchScalarGridSpec(
            num_scalar_prefetch=1,
            grid=(user_rows // CHUNK,),
            in_specs=[tile, tile, pl.BlockSpec((CHUNK, rank), lambda i, at: (i, 0)), IN_VMEM],
            out_specs=[IN_VMEM, IN_VMEM],
        ),
        compiler_params=SMALL,
        name="prepare",
    )(at, observed, ratings, start, held)


def stratum_errors(at, pieces, users, coded):
    ring = len(pieces)
    rows, rank = pieces[0].shape
    user_rows, items = coded.shape

    def body(*refs):
        errors_kernel(ring, *refs)

    out = pl.pallas_call(
        body,
        out_shape=[jax.ShapeDtypeStruct((user_rows, items), jnp.bfloat16)]
        + [jax.ShapeDtypeStruct((rows, rank), jnp.float32)] * ring
        + [jax.ShapeDtypeStruct((items, rank), jnp.bfloat16)],
        in_specs=[pl.BlockSpec(memory_space=pltpu.SMEM)] + [IN_VMEM] * (ring + 2),
        out_specs=[IN_VMEM] * (ring + 2),
        scratch_shapes=[pltpu.VMEM((rank, items), jnp.float32)],
        compiler_params=SMALL,
        name="errors",
    )(at, *pieces, users, coded)
    return out[0], out[1 : 1 + ring], out[1 + ring]


def users_update(items, errors, users, noise, user_rate):
    def body(*refs):
        users_kernel(user_rate, *refs)

    return pl.pallas_call(
        body,
        out_shape=jax.ShapeDtypeStruct(users.shape, jnp.float32),
        in_specs=[IN_VMEM] * 4,
        out_specs=IN_VMEM,
        compiler_params=SMALL,
        name="users",
    )(items, errors, users, noise)


def local(user_factors, item_factors, ratings, observed, plan, user_noise, item_noise):
    blk, shard = lax.axis_size("blk"), lax.axis_size("shard")
    ring = shard // TWINS
    user_rows = user_factors.shape[0]
    piece_rows = item_factors.shape[0]
    rows = piece_rows * TWINS
    user_rate = user_scale / ratings.shape[2]
    item_rate = item_scale / (shard * user_rows)
    strata = ratings.shape[0]
    x = lax.axis_index("shard") // TWINS
    twin = lax.axis_index("shard") % TWINS

    steps = [plan[t] for t in range(strata)]
    steps.append((-sum(steps)) % blk)
    zeros = jnp.zeros_like(item_factors)
    share = jnp.where(
        twin == 0,
        jnp.concatenate([item_factors, zeros], 0),
        jnp.concatenate([zeros, item_factors], 0),
    )

    def one(t, users, items):
        half = items.astype(jnp.bfloat16)
        pieces = [half] + [moved(half, 0, k) for k in range(1, ring)]
        at = jnp.stack([t, x]).astype(jnp.int32)
        coded, users = prepare(at, observed, ratings, user_factors, users)
        errors, grads, gathered = stratum_errors(at, pieces, users, coded)
        arrived = [grads[0]] + [moved(grads[k], 0, k) for k in range(1, ring)]
        user_drift = lax.dynamic_index_in_dim(user_noise, t, keepdims=False)
        users = users_update(gathered, errors, users, user_drift, user_rate)
        noise = lax.dynamic_slice(item_noise, (t, x * rows, 0), (1, rows, item_noise.shape[2]))[0]
        kept = jnp.where(twin == 0, items - item_rate * prior * items + noise, 0.0)
        return users, kept + item_rate * sum(arrived[1:], arrived[0])

    def trip(t, carry):
        users, share = carry
        step = steps[strata]
        for k in range(strata):
            step = jnp.where(t == k, steps[k], step)
        items = rotated_sum(share, step)
        return lax.cond(t < strata, one, lambda t, users, items: (users, items), t, users, items)

    users, items = lax.fori_loop(0, strata + 1, trip, (jnp.zeros_like(user_factors), share))
    piece = lax.dynamic_slice_in_dim(items, twin * piece_rows, piece_rows, 0)
    return users, piece


def solution(mesh):
    in_specs = (
        P(("blk", "shard"), None),
        P(("blk", "shard"), None),
        P(None, ("blk", "shard"), None),
        P(None, ("blk", "shard"), None),
        P(),
        P(None, ("blk", "shard"), None),
        P(None, "blk", None),
    )
    out_specs = (P(("blk", "shard"), None), P(("blk", "shard"), None))
    return jax.shard_map(local, mesh=mesh, in_specs=in_specs, out_specs=out_specs, check_vma=False)
```

```python
import jax
import jax.numpy as jnp
from jax import lax
from jax.experimental import pallas as pl
from jax.experimental.pallas import tpu as pltpu
from jax.sharding import PartitionSpec as P


user_scale = 12.0
item_scale = 30.0
prior = 1.0

FLAT = ("blk", "shard")
TWINS = 2
LOW = 8
CHUNK = 256
UNSEEN = 2.0**20


def pairs(blk, shard, distance, x_step):
    ring = shard // TWINS
    out = []
    for b in range(blk):
        for s in range(shard):
            x, twin = s // TWINS, s % TWINS
            far = (twin * blk + b + distance) % (TWINS * blk)
            to = ((x + x_step) % ring) * TWINS + far // blk
            out.append((b * shard + s, (far % blk) * shard + to))
    return out


def moved(value, distance, x_step=0):
    blk, shard = lax.axis_size("blk"), lax.axis_size("shard")
    if distance % (TWINS * blk) == 0 and x_step == 0:
        return value
    return lax.ppermute(value, FLAT, pairs(blk, shard, distance, x_step))


def digits(steps, blk):
    low = (steps + LOW // 2) % LOW
    return low, ((steps - (low - LOW // 2)) % blk) // LOW


def rotated(value, low, high):
    blk = lax.axis_size("blk")

    def first(d):
        return lambda v: moved(v, d)

    def second(d):
        return lambda v: (moved(v, d), moved(v, d + blk))

    value = lax.switch(low, [first(d - LOW // 2) for d in range(LOW)], value)
    return lax.switch(high, [second(d * LOW) for d in range(blk // LOW)], value)


def prepare_kernel(observed_ref, ratings_ref, coded_ref):
    rows = pl.ds(pl.multiple_of(pl.program_id(0) * CHUNK, CHUNK), CHUNK)
    ratings = ratings_ref[0].astype(jnp.float32)
    coded_ref[rows, :] = jnp.where(observed_ref[0] != 0, ratings, UNSEEN).astype(jnp.bfloat16)


def first_items(ring, at_ref, pieces, items_ref):
    for twin, piece in enumerate(pieces):
        side = at_ref[2] if twin == 0 else 1 - at_ref[2]
        rows = piece.shape[0] // ring
        for k in range(ring):
            place = (lax.rem(at_ref[0] + ring - k, ring) * TWINS + side) * rows
            items_ref[pl.ds(pl.multiple_of(place, rows), rows), :] = piece[k * rows : (k + 1) * rows, :]


def later_items(ring, at_ref, pieces, items_ref):
    for k in range(ring):
        rows = pieces[k].shape[0]
        place = lax.rem(at_ref[0] + ring - k, ring) * rows
        items_ref[pl.ds(pl.multiple_of(place, rows), rows), :] = pieces[k][...]


def errors_kernel(ring, put_items, count, at_ref, *refs):
    pieces, refs = refs[:count], refs[count:]
    users_ref, coded_ref, errors_ref = refs[:3]
    grads, items_ref, sum_ref = refs[3 : 3 + ring], refs[3 + ring], refs[4 + ring]
    put_items(ring, at_ref, pieces, items_ref)
    items = items_ref[...]
    total = None
    for c in range(users_ref.shape[0] // CHUNK):
        at = pl.ds(c * CHUNK, CHUNK)
        users_half = users_ref[at, :].astype(jnp.bfloat16)
        predicted = lax.dot_general(
            users_half, items, (((1,), (1,)), ((), ())), preferred_element_type=jnp.float32
        )
        coded = coded_ref[at, :].astype(jnp.float32)
        errors = jnp.where(coded < 0.5 * UNSEEN, coded - predicted, 0.0).astype(jnp.bfloat16)
        errors_ref[at, :] = errors
        part = lax.dot_general(
            users_half, errors, (((0,), (0,)), ((), ())), preferred_element_type=jnp.float32
        )
        total = part if total is None else total + part
    sum_ref[...] = total
    rows = items.shape[0] // ring
    for k in range(ring):
        place = lax.rem(at_ref[0] + k, ring) * rows
        grads[k][...] = sum_ref[:, pl.ds(pl.multiple_of(place, rows), rows)].T


def users_kernel(user_rate, items_ref, errors_ref, users_ref, noise_ref, out_ref):
    items = items_ref[...]
    for c in range(users_ref.shape[0] // CHUNK):
        at = pl.ds(c * CHUNK, CHUNK)
        users = users_ref[at, :]
        grad = jnp.dot(errors_ref[at, :], items, preferred_element_type=jnp.float32)
        out_ref[at, :] = users + user_rate * (grad - prior * users) + noise_ref[at, :]


def share_kernel(item_rate, whole, at_ref, items_ref, noise_ref, *refs):
    grads, out_ref = refs[:-1], refs[-1]
    rows = noise_ref.shape[0]
    if whole:
        items = items_ref[pl.ds(pl.multiple_of(at_ref[0] * rows, rows), rows), :].astype(jnp.float32)
    else:
        items = items_ref[...]
    grad = grads[0][...]
    for other in grads[1:]:
        grad = grad + other[...]
    kept = items - item_rate * prior * items + noise_ref[...]
    share = jnp.where(at_ref[1] == 0, kept, 0.0) + item_rate * grad
    high = share.astype(jnp.bfloat16)
    out_ref[0:rows, :] = high
    out_ref[rows : 2 * rows, :] = (share - high.astype(jnp.float32)).astype(jnp.bfloat16)


SMALL = pltpu.CompilerParams(vmem_limit_bytes=12 * 2**20)
IN_VMEM = pl.BlockSpec(memory_space=pltpu.VMEM)
IN_SMEM = pl.BlockSpec(memory_space=pltpu.SMEM)


def prepare(stratum, observed, ratings):
    _, user_rows, items = ratings.shape
    tile = pl.BlockSpec((1, CHUNK, items), lambda i: (stratum, i, 0))
    return pl.pallas_call(
        prepare_kernel,
        out_shape=jax.ShapeDtypeStruct((user_rows, items), jnp.bfloat16),
        grid=(user_rows // CHUNK,),
        in_specs=[tile, tile],
        out_specs=IN_VMEM,
        compiler_params=SMALL,
        name="prepare",
    )(observed, ratings)


def stratum_errors(put_items, ring, at, pieces, users, coded):
    user_rows, items = coded.shape
    rank = users.shape[1]
    rows = items // ring

    def body(*refs):
        errors_kernel(ring, put_items, len(pieces), *refs)

    out = pl.pallas_call(
        body,
        out_shape=[jax.ShapeDtypeStruct((user_rows, items), jnp.bfloat16)]
        + [jax.ShapeDtypeStruct((rows, rank), jnp.float32)] * ring
        + [jax.ShapeDtypeStruct((items, rank), jnp.bfloat16)],
        in_specs=[IN_SMEM] + [IN_VMEM] * (len(pieces) + 2),
        out_specs=[IN_VMEM] * (ring + 2),
        scratch_shapes=[pltpu.VMEM((rank, items), jnp.float32)],
        compiler_params=SMALL,
        name="errors",
    )(at, *pieces, users, coded)
    return out[0], out[1 : 1 + ring], out[1 + ring]


def users_update(items, errors, users, noise, user_rate):
    def body(*refs):
        users_kernel(user_rate, *refs)

    return pl.pallas_call(
        body,
        out_shape=jax.ShapeDtypeStruct(users.shape, jnp.float32),
        in_specs=[IN_VMEM] * 4,
        out_specs=IN_VMEM,
        compiler_params=SMALL,
        name="users",
    )(items, errors, users, noise)


def packed_share(at, items, noise, grads, item_rate):
    rows, rank = noise.shape
    whole = items.shape[0] != rows

    def body(*refs):
        share_kernel(item_rate, whole, *refs)

    return pl.pallas_call(
        body,
        out_shape=jax.ShapeDtypeStruct((2 * rows, rank), jnp.bfloat16),
        in_specs=[IN_SMEM] + [IN_VMEM] * (2 + len(grads)),
        out_specs=IN_VMEM,
        compiler_params=SMALL,
        name="share",
    )(at, items, noise, *grads)


def added(own, other):
    rows = own.shape[0] // 2
    own, other = own.astype(jnp.float32), other.astype(jnp.float32)
    return (own[:rows] + own[rows:]) + (other[:rows] + other[rows:])


def local(user_factors, item_factors, ratings, observed, plan, user_noise, item_noise):
    blk, shard = lax.axis_size("blk"), lax.axis_size("shard")
    ring = shard // TWINS
    user_rows = user_factors.shape[0]
    piece_rows, rank = item_factors.shape
    rows = piece_rows * TWINS
    user_rate = user_scale / ratings.shape[2]
    item_rate = item_scale / (shard * user_rows)
    strata = ratings.shape[0]
    x = lax.axis_index("shard") // TWINS
    twin = lax.axis_index("shard") % TWINS
    place = twin * blk + lax.axis_index("blk")

    steps = [plan[t] for t in range(strata)]
    steps.append((-sum(steps)) % blk)
    low0, high0 = digits(steps[0], blk)
    side = ((place - (low0 - LOW // 2) - LOW * high0) % (TWINS * blk)) // blk
    at = jnp.stack([x, twin, side]).astype(jnp.int32)

    rounded = item_factors.astype(jnp.bfloat16)
    start = jnp.concatenate([rounded] + [moved(rounded, 0, k) for k in range(1, ring)], 0)
    coded0 = prepare(0, observed, ratings)

    def work(t, put_items, pieces, items, users, coded):
        noise = lax.dynamic_slice(item_noise[t], (x * rows, 0), (rows, rank))
        errors, grads, gathered = stratum_errors(put_items, ring, at, pieces, users, coded)
        arrived = [grads[0]] + [moved(grads[k], 0, k) for k in range(1, ring)]
        users = users_update(gathered, errors, users, user_noise[t], user_rate)
        share = packed_share(at, gathered if items is None else items, noise, arrived, item_rate)
        return users, share

    def first(users, final, own, other):
        return *work(0, first_items, [own, other], None, user_factors, coded0), final

    def later(t):
        def branch(users, final, own, other):
            items = added(own, other)
            half = items.astype(jnp.bfloat16)
            pieces = [half] + [moved(half, 0, k) for k in range(1, ring)]
            coded = prepare(t, observed, ratings)
            return *work(t, later_items, pieces, items, users, coded), final

        return branch

    def last(users, final, own, other):
        return users, own, added(own, other)

    branches = [first] + [later(t) for t in range(1, strata)] + [last]

    def trip(t, carry):
        users, value, final = carry
        step = steps[strata]
        for k in range(strata):
            step = jnp.where(t == k, steps[k], step)
        own, other = rotated(value, *digits(step, blk))
        return lax.switch(t, branches, users, final, own, other)

    held = (jnp.zeros_like(user_factors), start, jnp.zeros((rows, rank), jnp.float32))
    users, _, final = lax.fori_loop(0, strata + 1, trip, held)
    piece = lax.dynamic_slice_in_dim(final, twin * piece_rows, piece_rows, 0)
    kept = (1.0 - item_rate * prior) ** strata
    return users, piece + kept * (item_factors - rounded.astype(jnp.float32))


def solution(mesh):
    in_specs = (
        P(("blk", "shard"), None),
        P(("blk", "shard"), None),
        P(None, ("blk", "shard"), None),
        P(None, ("blk", "shard"), None),
        P(),
        P(None, ("blk", "shard"), None),
        P(None, "blk", None),
    )
    out_specs = (P(("blk", "shard"), None), P(("blk", "shard"), None))
    return jax.shard_map(local, mesh=mesh, in_specs=in_specs, out_specs=out_specs, check_vma=False)
```

```python
import jax
import jax.numpy as jnp
from jax import lax
from jax.experimental import pallas as pl
from jax.experimental.pallas import tpu as pltpu
from jax.sharding import PartitionSpec as P


user_scale = 12.0
item_scale = 30.0
prior = 1.0

FLAT = ("blk", "shard")
TWINS = 2
CHUNK = 256
UNSEEN = 2.0**20


def pairs(blk, shard, distance, x_step):
    ring = shard // TWINS
    out = []
    for b in range(blk):
        for s in range(shard):
            x, twin = s // TWINS, s % TWINS
            far = (twin * blk + b + distance) % (TWINS * blk)
            to = ((x + x_step) % ring) * TWINS + far // blk
            out.append((b * shard + s, (far % blk) * shard + to))
    return out


def moved(value, distance, x_step=0):
    blk, shard = lax.axis_size("blk"), lax.axis_size("shard")
    if distance % (TWINS * blk) == 0 and x_step == 0:
        return value
    return lax.ppermute(value, FLAT, pairs(blk, shard, distance, x_step))


def rotated(share, steps):
    blk = lax.axis_size("blk")

    def branch(d):
        return lambda v: moved(v, d)

    return lax.switch(steps, [branch(d if d < blk // 2 else d - blk) for d in range(blk)], share)


def prepare_kernel(at_ref, observed_ref, ratings_ref, start_ref, held_ref, coded_ref, users_ref):
    step = pl.program_id(0)
    rows = pl.ds(pl.multiple_of(step * CHUNK, CHUNK), CHUNK)
    ratings = ratings_ref[0].astype(jnp.float32)
    coded_ref[rows, :] = jnp.where(observed_ref[0] != 0, ratings, UNSEEN).astype(jnp.bfloat16)

    @pl.when(at_ref[0] == 0)
    def _():
        users_ref[rows, :] = start_ref[...]

    @pl.when(at_ref[0] != 0)
    def _():
        users_ref[rows, :] = held_ref[rows, :]


def errors_kernel(ring, at_ref, *refs):
    pieces, refs = refs[:ring], refs[ring:]
    users_ref, coded_ref, errors_ref = refs[:3]
    grads, items_ref, sum_ref = refs[3 : 3 + ring], refs[3 + ring], refs[4 + ring]
    rows = pieces[0].shape[0]
    x = at_ref[1]
    for k in range(ring):
        place = lax.rem(x + ring - k, ring) * rows
        items_ref[pl.ds(pl.multiple_of(place, rows), rows), :] = pieces[k][...]
    items = items_ref[...]
    total = None
    for c in range(users_ref.shape[0] // CHUNK):
        at = pl.ds(c * CHUNK, CHUNK)
        users_half = users_ref[at, :].astype(jnp.bfloat16)
        predicted = lax.dot_general(
            users_half, items, (((1,), (1,)), ((), ())), preferred_element_type=jnp.float32
        )
        coded = coded_ref[at, :].astype(jnp.float32)
        errors = jnp.where(coded < 0.5 * UNSEEN, coded - predicted, 0.0).astype(jnp.bfloat16)
        errors_ref[at, :] = errors
        part = lax.dot_general(
            users_half, errors, (((0,), (0,)), ((), ())), preferred_element_type=jnp.float32
        )
        total = part if total is None else total + part
    sum_ref[...] = total
    for k in range(ring):
        place = lax.rem(x + k, ring) * rows
        grads[k][...] = sum_ref[:, pl.ds(pl.multiple_of(place, rows), rows)].T


def users_kernel(user_rate, items_ref, errors_ref, users_ref, noise_ref, out_ref):
    items = items_ref[...]
    for c in range(users_ref.shape[0] // CHUNK):
        at = pl.ds(c * CHUNK, CHUNK)
        users = users_ref[at, :]
        grad = jnp.dot(errors_ref[at, :], items, preferred_element_type=jnp.float32)
        out_ref[at, :] = users + user_rate * (grad - prior * users) + noise_ref[at, :]


SMALL = pltpu.CompilerParams(vmem_limit_bytes=12 * 2**20)
IN_VMEM = pl.BlockSpec(memory_space=pltpu.VMEM)


def prepare(at, observed, ratings, start, held):
    user_rows, rank = start.shape
    items = ratings.shape[2]
    tile = pl.BlockSpec((1, CHUNK, items), lambda i, at: (at[0], i, 0))
    return pl.pallas_call(
        prepare_kernel,
        out_shape=[
            jax.ShapeDtypeStruct((user_rows, items), jnp.bfloat16),
            jax.ShapeDtypeStruct((user_rows, rank), jnp.float32),
        ],
        grid_spec=pltpu.PrefetchScalarGridSpec(
            num_scalar_prefetch=1,
            grid=(user_rows // CHUNK,),
            in_specs=[tile, tile, pl.BlockSpec((CHUNK, rank), lambda i, at: (i, 0)), IN_VMEM],
            out_specs=[IN_VMEM, IN_VMEM],
        ),
        compiler_params=SMALL,
        name="prepare",
    )(at, observed, ratings, start, held)


def stratum_errors(at, pieces, users, coded):
    ring = len(pieces)
    rows, rank = pieces[0].shape
    user_rows, items = coded.shape

    def body(*refs):
        errors_kernel(ring, *refs)

    out = pl.pallas_call(
        body,
        out_shape=[jax.ShapeDtypeStruct((user_rows, items), jnp.bfloat16)]
        + [jax.ShapeDtypeStruct((rows, rank), jnp.float32)] * ring
        + [jax.ShapeDtypeStruct((items, rank), jnp.bfloat16)],
        in_specs=[pl.BlockSpec(memory_space=pltpu.SMEM)] + [IN_VMEM] * (ring + 2),
        out_specs=[IN_VMEM] * (ring + 2),
        scratch_shapes=[pltpu.VMEM((rank, items), jnp.float32)],
        compiler_params=SMALL,
        name="errors",
    )(at, *pieces, users, coded)
    return out[0], out[1 : 1 + ring], out[1 + ring]


def users_update(items, errors, users, noise, user_rate):
    def body(*refs):
        users_kernel(user_rate, *refs)

    return pl.pallas_call(
        body,
        out_shape=jax.ShapeDtypeStruct(users.shape, jnp.float32),
        in_specs=[IN_VMEM] * 4,
        out_specs=IN_VMEM,
        compiler_params=SMALL,
        name="users",
    )(items, errors, users, noise)


def local(user_factors, item_factors, ratings, observed, plan, user_noise, item_noise):
    blk, shard = lax.axis_size("blk"), lax.axis_size("shard")
    ring = shard // TWINS
    user_rows = user_factors.shape[0]
    piece_rows = item_factors.shape[0]
    rows = piece_rows * TWINS
    user_rate = user_scale / ratings.shape[2]
    item_rate = item_scale / (shard * user_rows)
    strata = ratings.shape[0]
    x = lax.axis_index("shard") // TWINS
    twin = lax.axis_index("shard") % TWINS

    steps = [plan[t] for t in range(strata)]
    steps.append((-sum(steps)) % blk)
    zeros = jnp.zeros_like(item_factors)
    share = jnp.where(
        twin == 0,
        jnp.concatenate([item_factors, zeros], 0),
        jnp.concatenate([zeros, item_factors], 0),
    )

    def one(t, users, share):
        at = jnp.stack([t, x]).astype(jnp.int32)
        noise = lax.dynamic_slice(item_noise, (t, x * rows, 0), (1, rows, item_noise.shape[2]))[0]
        flipped = moved(share, blk)
        coded, users = prepare(at, observed, ratings, user_factors, users)
        flipped, coded, users, noise = lax.optimization_barrier((flipped, coded, users, noise))
        items = share + flipped
        half = items.astype(jnp.bfloat16)
        pieces = [half] + [moved(half, 0, k) for k in range(1, ring)]
        drift = lax.dynamic_index_in_dim(user_noise, t, keepdims=False)
        kept = jnp.where(twin == 0, items - item_rate * prior * items + noise, 0.0)
        errors, grads, gathered = stratum_errors(at, pieces, users, coded)
        arrived = [grads[0]] + [moved(grads[k], 0, k) for k in range(1, ring)]
        users = users_update(gathered, errors, users, drift, user_rate)
        return users, kept + item_rate * sum(arrived[1:], arrived[0])

    def none(t, users, share):
        return users, share + moved(share, blk)

    def trip(t, carry):
        users, share = carry
        step = steps[strata]
        for k in range(strata):
            step = jnp.where(t == k, steps[k], step)
        return lax.cond(t < strata, one, none, t, users, rotated(share, step))

    users, items = lax.fori_loop(0, strata + 1, trip, (jnp.zeros_like(user_factors), share))
    piece = lax.dynamic_slice_in_dim(items, twin * piece_rows, piece_rows, 0)
    return users, piece


def solution(mesh):
    in_specs = (
        P(("blk", "shard"), None),
        P(("blk", "shard"), None),
        P(None, ("blk", "shard"), None),
        P(None, ("blk", "shard"), None),
        P(),
        P(None, ("blk", "shard"), None),
        P(None, "blk", None),
    )
    out_specs = (P(("blk", "shard"), None), P(("blk", "shard"), None))
    return jax.shard_map(local, mesh=mesh, in_specs=in_specs, out_specs=out_specs, check_vma=False)
```

```python
import jax
import jax.numpy as jnp
from jax import lax
from jax.experimental import pallas as pl
from jax.experimental.pallas import tpu as pltpu
from jax.sharding import PartitionSpec as P


user_scale = 12.0
item_scale = 30.0
prior = 1.0

FLAT = ("blk", "shard")
TWINS = 2
CHUNK = 256
UNSEEN = 2.0**20


def pairs(blk, shard, distance, x_step):
    ring = shard // TWINS
    out = []
    for b in range(blk):
        for s in range(shard):
            x, twin = s // TWINS, s % TWINS
            far = (twin * blk + b + distance) % (TWINS * blk)
            to = ((x + x_step) % ring) * TWINS + far // blk
            out.append((b * shard + s, (far % blk) * shard + to))
    return out


def moved(value, distance, x_step=0):
    blk, shard = lax.axis_size("blk"), lax.axis_size("shard")
    if distance % (TWINS * blk) == 0 and x_step == 0:
        return value
    return lax.ppermute(value, FLAT, pairs(blk, shard, distance, x_step))


def rotated(share, steps):
    blk = lax.axis_size("blk")

    def branch(d):
        return lambda v: moved(v, d)

    return lax.switch(steps, [branch(d if d < blk // 2 else d - blk) for d in range(blk)], share)


def prepare_kernel(at_ref, observed_ref, ratings_ref, start_ref, held_ref, coded_ref, users_ref):
    step = pl.program_id(0)
    rows = pl.ds(pl.multiple_of(step * CHUNK, CHUNK), CHUNK)
    ratings = ratings_ref[0].astype(jnp.float32)
    coded_ref[rows, :] = jnp.where(observed_ref[0] != 0, ratings, UNSEEN).astype(jnp.bfloat16)

    @pl.when(at_ref[0] == 0)
    def _():
        users_ref[rows, :] = start_ref[...]

    @pl.when(at_ref[0] != 0)
    def _():
        users_ref[rows, :] = held_ref[rows, :]


def errors_kernel(back, at_ref, piece_ref, users_ref, coded_ref, errors_ref, grad_ref):
    rows = piece_ref.shape[0]
    ring = coded_ref.shape[1] // rows
    place = pl.multiple_of(lax.rem(at_ref[1] + ring - back, ring) * rows, rows)
    piece = piece_ref[...]
    total = None
    for c in range(users_ref.shape[0] // CHUNK):
        at = pl.ds(c * CHUNK, CHUNK)
        users_half = users_ref[at, :].astype(jnp.bfloat16)
        predicted = lax.dot_general(
            users_half, piece, (((1,), (1,)), ((), ())), preferred_element_type=jnp.float32
        )
        coded = coded_ref[at, pl.ds(place, rows)].astype(jnp.float32)
        errors = jnp.where(coded < 0.5 * UNSEEN, coded - predicted, 0.0).astype(jnp.bfloat16)
        errors_ref[at, :] = errors
        part = lax.dot_general(
            errors, users_half, (((0,), (0,)), ((), ())), preferred_element_type=jnp.float32
        )
        total = part if total is None else total + part
    grad_ref[...] = total


def users_kernel(user_rate, ring, *refs):
    pieces, errors, (users_ref, noise_ref, out_ref) = refs[:ring], refs[ring : 2 * ring], refs[2 * ring :]
    for c in range(users_ref.shape[0] // CHUNK):
        at = pl.ds(c * CHUNK, CHUNK)
        users = users_ref[at, :]
        grad = None
        for piece, error in zip(pieces, errors):
            part = jnp.dot(error[at, :], piece[...], preferred_element_type=jnp.float32)
            grad = part if grad is None else grad + part
        out_ref[at, :] = users + user_rate * (grad - prior * users) + noise_ref[at, :]


SMALL = pltpu.CompilerParams(vmem_limit_bytes=12 * 2**20)
IN_VMEM = pl.BlockSpec(memory_space=pltpu.VMEM)


def prepare(at, observed, ratings, start, held):
    user_rows, rank = start.shape
    items = ratings.shape[2]
    tile = pl.BlockSpec((1, CHUNK, items), lambda i, at: (at[0], i, 0))
    return pl.pallas_call(
        prepare_kernel,
        out_shape=[
            jax.ShapeDtypeStruct((user_rows, items), jnp.bfloat16),
            jax.ShapeDtypeStruct((user_rows, rank), jnp.float32),
        ],
        grid_spec=pltpu.PrefetchScalarGridSpec(
            num_scalar_prefetch=1,
            grid=(user_rows // CHUNK,),
            in_specs=[tile, tile, pl.BlockSpec((CHUNK, rank), lambda i, at: (i, 0)), IN_VMEM],
            out_specs=[IN_VMEM, IN_VMEM],
        ),
        compiler_params=SMALL,
        name="prepare",
    )(at, observed, ratings, start, held)


def piece_errors(back, at, piece, users, coded):
    user_rows = users.shape[0]
    rows, rank = piece.shape

    def body(*refs):
        errors_kernel(back, *refs)

    return pl.pallas_call(
        body,
        out_shape=[
            jax.ShapeDtypeStruct((user_rows, rows), jnp.bfloat16),
            jax.ShapeDtypeStruct((rows, rank), jnp.float32),
        ],
        in_specs=[pl.BlockSpec(memory_space=pltpu.SMEM)] + [IN_VMEM] * 3,
        out_specs=[IN_VMEM] * 2,
        compiler_params=SMALL,
        name=f"errors{back}",
    )(at, piece, users, coded)


def users_update(pieces, errors, users, noise, user_rate):
    ring = len(pieces)

    def body(*refs):
        users_kernel(user_rate, ring, *refs)

    return pl.pallas_call(
        body,
        out_shape=jax.ShapeDtypeStruct(users.shape, jnp.float32),
        in_specs=[IN_VMEM] * (2 * ring + 2),
        out_specs=IN_VMEM,
        compiler_params=SMALL,
        name="users",
    )(*pieces, *errors, users, noise)


def local(user_factors, item_factors, ratings, observed, plan, user_noise, item_noise):
    blk, shard = lax.axis_size("blk"), lax.axis_size("shard")
    ring = shard // TWINS
    user_rows = user_factors.shape[0]
    piece_rows = item_factors.shape[0]
    rows = piece_rows * TWINS
    user_rate = user_scale / ratings.shape[2]
    item_rate = item_scale / (shard * user_rows)
    strata = ratings.shape[0]
    x = lax.axis_index("shard") // TWINS
    twin = lax.axis_index("shard") % TWINS

    steps = [plan[t] for t in range(strata)]
    steps.append(lax.rem(strata * blk - sum(steps), blk))
    zeros = jnp.zeros_like(item_factors)
    share = jnp.where(
        twin == 0,
        jnp.concatenate([item_factors, zeros], 0),
        jnp.concatenate([zeros, item_factors], 0),
    )

    def one(t, users, share):
        at = jnp.stack([t, x]).astype(jnp.int32)
        noise = lax.dynamic_slice(item_noise, (t, x * rows, 0), (1, rows, item_noise.shape[2]))[0]
        flipped = moved(share, blk)
        coded, users = prepare(at, observed, ratings, user_factors, users)
        flipped, coded, users, noise = lax.optimization_barrier((flipped, coded, users, noise))
        items = share + flipped
        half = items.astype(jnp.bfloat16)
        order = sorted(range(1, ring), key=lambda k: min(k, ring - k))
        away = {k: moved(half, 0, k) for k in order}
        drift = lax.dynamic_index_in_dim(user_noise, t, keepdims=False)
        kept = jnp.where(twin == 0, items - item_rate * prior * items + noise, 0.0)
        pieces, errors, total = [half], [], None
        error, total = piece_errors(0, at, half, users, coded)
        errors = [error]
        for k in order:
            error, grad = piece_errors(k, at, away[k], users, coded)
            pieces.append(away[k])
            errors.append(error)
            total = total + moved(grad, 0, -k)
        users = users_update(pieces, errors, users, drift, user_rate)
        return users, kept + item_rate * total

    def none(t, users, share):
        return users, share + moved(share, blk)

    def trip(t, carry):
        users, share = carry
        step = steps[strata]
        for k in range(strata):
            step = jnp.where(t == k, steps[k], step)
        return lax.cond(t < strata, one, none, t, users, rotated(share, step))

    users, items = lax.fori_loop(0, strata + 1, trip, (jnp.zeros_like(user_factors), share))
    piece = lax.dynamic_slice_in_dim(items, twin * piece_rows, piece_rows, 0)
    return users, piece


def solution(mesh):
    in_specs = (
        P(("blk", "shard"), None),
        P(("blk", "shard"), None),
        P(None, ("blk", "shard"), None),
        P(None, ("blk", "shard"), None),
        P(),
        P(None, ("blk", "shard"), None),
        P(None, "blk", None),
    )
    out_specs = (P(("blk", "shard"), None), P(("blk", "shard"), None))
    return jax.shard_map(local, mesh=mesh, in_specs=in_specs, out_specs=out_specs, check_vma=False)
```

```python
import jax
import jax.numpy as jnp
from jax import lax
from jax.experimental import pallas as pl
from jax.experimental.pallas import tpu as pltpu
from jax.sharding import PartitionSpec as P


user_scale = 12.0
item_scale = 30.0
prior = 1.0

FLAT = ("blk", "shard")
TWINS = 2
CHUNK = 256
UNSEEN = 2.0**20


def pairs(blk, shard, distance, x_step):
    ring = shard // TWINS
    out = []
    for b in range(blk):
        for s in range(shard):
            x, twin = s // TWINS, s % TWINS
            far = (twin * blk + b + distance) % (TWINS * blk)
            to = ((x + x_step) % ring) * TWINS + far // blk
            out.append((b * shard + s, (far % blk) * shard + to))
    return out


def moved(value, distance, x_step=0):
    blk, shard = lax.axis_size("blk"), lax.axis_size("shard")
    if distance % (TWINS * blk) == 0 and x_step == 0:
        return value
    return lax.ppermute(value, FLAT, pairs(blk, shard, distance, x_step))


def rotated(share, steps):
    blk = lax.axis_size("blk")

    def branch(d):
        return lambda v: moved(v, d)

    return lax.switch(steps, [branch(d if d < blk // 2 else d - blk) for d in range(blk)], share)


def prepare_kernel(
    at_ref, observed_ref, ratings_ref, start_ref, held_ref, coded_ref, users_ref, half_ref, turned_ref
):
    step = pl.program_id(0)
    rows = pl.ds(pl.multiple_of(step * CHUNK, CHUNK), CHUNK)
    ratings = ratings_ref[0].astype(jnp.float32)
    coded_ref[rows, :] = jnp.where(observed_ref[0] != 0, ratings, UNSEEN).astype(jnp.bfloat16)

    @pl.when(at_ref[0] == 0)
    def _():
        users_ref[rows, :] = start_ref[...]

    @pl.when(at_ref[0] != 0)
    def _():
        users_ref[rows, :] = held_ref[rows, :]

    half = users_ref[rows, :].astype(jnp.bfloat16)
    half_ref[rows, :] = half
    turned_ref[:, rows] = half.T


def errors_kernel(back, piece_ref, half_ref, turned_ref, coded_ref, errors_ref, grad_ref):
    rows = piece_ref.shape[0]
    ring = coded_ref.shape[1] // rows
    x = lax.axis_index("shard") // TWINS
    place = pl.multiple_of(lax.rem(x + ring - back, ring) * rows, rows)
    piece = piece_ref[...]
    for c in range(half_ref.shape[0] // CHUNK):
        at = pl.ds(c * CHUNK, CHUNK)
        predicted = lax.dot_general(
            half_ref[at, :], piece, (((1,), (1,)), ((), ())), preferred_element_type=jnp.float32
        )
        coded = coded_ref[at, pl.ds(place, rows)].astype(jnp.float32)
        errors = jnp.where(coded < 0.5 * UNSEEN, coded - predicted, 0.0)
        errors_ref[at, :] = errors.astype(jnp.bfloat16)
    grad = jnp.dot(turned_ref[...], errors_ref[...], preferred_element_type=jnp.float32)
    grad_ref[...] = grad.T


def users_kernel(user_rate, ring, *refs):
    pieces, errors, (users_ref, noise_ref, out_ref) = refs[:ring], refs[ring : 2 * ring], refs[2 * ring :]
    for c in range(users_ref.shape[0] // CHUNK):
        at = pl.ds(c * CHUNK, CHUNK)
        users = users_ref[at, :]
        grad = None
        for piece, error in zip(pieces, errors):
            part = jnp.dot(error[at, :], piece[...], preferred_element_type=jnp.float32)
            grad = part if grad is None else grad + part
        out_ref[at, :] = users + user_rate * (grad - prior * users) + noise_ref[at, :]


SMALL = pltpu.CompilerParams(vmem_limit_bytes=12 * 2**20)
IN_VMEM = pl.BlockSpec(memory_space=pltpu.VMEM)


def prepare(at, observed, ratings, start, held):
    user_rows, rank = start.shape
    items = ratings.shape[2]
    tile = pl.BlockSpec((1, CHUNK, items), lambda i, at: (at[0], i, 0))
    return pl.pallas_call(
        prepare_kernel,
        out_shape=[
            jax.ShapeDtypeStruct((user_rows, items), jnp.bfloat16),
            jax.ShapeDtypeStruct((user_rows, rank), jnp.float32),
            jax.ShapeDtypeStruct((user_rows, rank), jnp.bfloat16),
            jax.ShapeDtypeStruct((rank, user_rows), jnp.bfloat16),
        ],
        grid_spec=pltpu.PrefetchScalarGridSpec(
            num_scalar_prefetch=1,
            grid=(user_rows // CHUNK,),
            in_specs=[tile, tile, pl.BlockSpec((CHUNK, rank), lambda i, at: (i, 0)), IN_VMEM],
            out_specs=[IN_VMEM] * 4,
        ),
        compiler_params=SMALL,
        name="prepare",
    )(at, observed, ratings, start, held)


def piece_errors(back, piece, half, turned, coded):
    user_rows = half.shape[0]
    rows, rank = piece.shape

    def body(*refs):
        errors_kernel(back, *refs)

    return pl.pallas_call(
        body,
        out_shape=[
            jax.ShapeDtypeStruct((user_rows, rows), jnp.bfloat16),
            jax.ShapeDtypeStruct((rows, rank), jnp.float32),
        ],
        in_specs=[IN_VMEM] * 4,
        out_specs=[IN_VMEM] * 2,
        compiler_params=SMALL,
        name=f"errors{back}",
    )(piece, half, turned, coded)


def users_update(pieces, errors, users, noise, user_rate):
    ring = len(pieces)

    def body(*refs):
        users_kernel(user_rate, ring, *refs)

    return pl.pallas_call(
        body,
        out_shape=jax.ShapeDtypeStruct(users.shape, jnp.float32),
        in_specs=[IN_VMEM] * (2 * ring + 2),
        out_specs=IN_VMEM,
        compiler_params=SMALL,
        name="users",
    )(*pieces, *errors, users, noise)


def local(user_factors, item_factors, ratings, observed, plan, user_noise, item_noise):
    blk, shard = lax.axis_size("blk"), lax.axis_size("shard")
    ring = shard // TWINS
    user_rows = user_factors.shape[0]
    piece_rows = item_factors.shape[0]
    rows = piece_rows * TWINS
    user_rate = user_scale / ratings.shape[2]
    item_rate = item_scale / (shard * user_rows)
    strata = ratings.shape[0]
    x = lax.axis_index("shard") // TWINS
    twin = lax.axis_index("shard") % TWINS

    steps = [plan[t] for t in range(strata)]
    steps.append(lax.rem(strata * blk - sum(steps), blk))
    zeros = jnp.zeros_like(item_factors)
    share = jnp.where(
        twin == 0,
        jnp.concatenate([item_factors, zeros], 0),
        jnp.concatenate([zeros, item_factors], 0),
    )

    def one(t, users, share):
        at = jnp.stack([t, x]).astype(jnp.int32)
        noise = lax.dynamic_slice(item_noise, (t, x * rows, 0), (1, rows, item_noise.shape[2]))[0]
        flipped = moved(share, blk)
        ready = prepare(at, observed, ratings, user_factors, users)
        flipped, ready, noise = lax.optimization_barrier((flipped, ready, noise))
        coded, users, users_half, turned = ready
        items = share + flipped
        half = items.astype(jnp.bfloat16)
        order = sorted(range(1, ring), key=lambda k: min(k, ring - k))
        away = {k: moved(half, 0, k) for k in order}
        drift = lax.dynamic_index_in_dim(user_noise, t, keepdims=False)
        kept = jnp.where(twin == 0, items - item_rate * prior * items + noise, 0.0)
        error, total = piece_errors(0, half, users_half, turned, coded)
        pieces, errors = [half], [error]
        for k in order:
            error, grad = piece_errors(k, away[k], users_half, turned, coded)
            pieces.append(away[k])
            errors.append(error)
            total = total + moved(grad, 0, -k)
        users = users_update(pieces, errors, users, drift, user_rate)
        return users, kept + item_rate * total

    def none(t, users, share):
        return users, share + moved(share, blk)

    def trip(t, carry):
        users, share = carry
        step = steps[strata]
        for k in range(strata):
            step = jnp.where(t == k, steps[k], step)
        return lax.cond(t < strata, one, none, t, users, rotated(share, step))

    users, items = lax.fori_loop(0, strata + 1, trip, (jnp.zeros_like(user_factors), share))
    piece = lax.dynamic_slice_in_dim(items, twin * piece_rows, piece_rows, 0)
    return users, piece


def solution(mesh):
    in_specs = (
        P(("blk", "shard"), None),
        P(("blk", "shard"), None),
        P(None, ("blk", "shard"), None),
        P(None, ("blk", "shard"), None),
        P(),
        P(None, ("blk", "shard"), None),
        P(None, "blk", None),
    )
    out_specs = (P(("blk", "shard"), None), P(("blk", "shard"), None))
    return jax.shard_map(local, mesh=mesh, in_specs=in_specs, out_specs=out_specs, check_vma=False)
```

```python
import jax
import jax.numpy as jnp
from jax import lax
from jax.experimental import pallas as pl
from jax.experimental.pallas import tpu as pltpu
from jax.sharding import PartitionSpec as P


user_scale = 12.0
item_scale = 30.0
prior = 1.0

FLAT = ("blk", "shard")
TWINS = 2
CHUNK = 256
UNSEEN = 2.0**20


def pairs(blk, shard, distance, x_step):
    ring = shard // TWINS
    out = []
    for b in range(blk):
        for s in range(shard):
            x, twin = s // TWINS, s % TWINS
            far = (twin * blk + b + distance) % (TWINS * blk)
            to = ((x + x_step) % ring) * TWINS + far // blk
            out.append((b * shard + s, (far % blk) * shard + to))
    return out


def moved(value, distance, x_step=0):
    blk, shard = lax.axis_size("blk"), lax.axis_size("shard")
    if distance % (TWINS * blk) == 0 and x_step == 0:
        return value
    return lax.ppermute(value, FLAT, pairs(blk, shard, distance, x_step))


def rotated(share, steps):
    blk = lax.axis_size("blk")

    def branch(d):
        return lambda v: moved(v, d)

    return lax.switch(steps, [branch(d if d < blk // 2 else d - blk) for d in range(blk)], share)


def start_kernel(strata, blk, plan_ref, items_ref, code_ref, at_ref, share_ref, room_ref):
    del room_ref
    bits = (blk - 1).bit_length()
    code, taken = 0, 0
    for t in range(strata):
        code = code + plan_ref[t] * (1 << (t * bits))
        taken = taken + plan_ref[t]
    back = lax.rem(strata * blk - taken, blk)
    code_ref[0] = code + back * (1 << (strata * bits)) + (1 << ((strata + 1) * bits))
    shard = lax.axis_index("shard")
    at_ref[0] = 0
    at_ref[1] = shard // TWINS
    rows = items_ref.shape[0]
    share_ref[...] = jnp.zeros_like(share_ref)
    place = pl.multiple_of(lax.rem(shard, TWINS) * rows, rows)
    share_ref[pl.ds(place, rows), :] = items_ref[...]


def prepare_kernel(
    user_rate,
    at_ref,
    observed_ref,
    ratings_ref,
    start_ref,
    held_ref,
    noise_ref,
    item_noise_ref,
    coded_ref,
    base_ref,
    half_ref,
    turned_ref,
    item_noise_out_ref,
):
    step = pl.program_id(0)
    rows = pl.ds(pl.multiple_of(step * CHUNK, CHUNK), CHUNK)
    ratings = ratings_ref[0].astype(jnp.float32)
    coded_ref[rows, :] = jnp.where(observed_ref[0] != 0, ratings, UNSEEN).astype(jnp.bfloat16)
    users = jnp.where(at_ref[0] == 0, start_ref[...], held_ref[...])
    base_ref[rows, :] = users - user_rate * prior * users + noise_ref[0]
    half = users.astype(jnp.bfloat16)
    half_ref[rows, :] = half
    turned_ref[:, rows] = half.T

    @pl.when(step == 0)
    def _():
        item_noise_out_ref[...] = item_noise_ref[0]


def errors_kernel(back, piece_ref, half_ref, turned_ref, coded_ref, errors_ref, grad_ref):
    rows = piece_ref.shape[0]
    ring = coded_ref.shape[1] // rows
    x = lax.axis_index("shard") // TWINS
    place = pl.multiple_of(lax.rem(x + ring - back, ring) * rows, rows)
    piece = piece_ref[...]
    for c in range(half_ref.shape[0] // CHUNK):
        at = pl.ds(c * CHUNK, CHUNK)
        predicted = lax.dot_general(
            half_ref[at, :], piece, (((1,), (1,)), ((), ())), preferred_element_type=jnp.float32
        )
        coded = coded_ref[at, pl.ds(place, rows)].astype(jnp.float32)
        errors = jnp.where(coded < 0.5 * UNSEEN, coded - predicted, 0.0)
        errors_ref[at, :] = errors.astype(jnp.bfloat16)
    grad = jnp.dot(turned_ref[...], errors_ref[...], preferred_element_type=jnp.float32)
    grad_ref[...] = grad.T


def users_kernel(user_rate, ring, *refs):
    pieces, errors, (base_ref, out_ref) = refs[:ring], refs[ring : 2 * ring], refs[2 * ring :]
    for c in range(base_ref.shape[0] // CHUNK):
        at = pl.ds(c * CHUNK, CHUNK)
        grad = None
        for piece, error in zip(pieces, errors):
            part = jnp.dot(error[at, :], piece[...], preferred_element_type=jnp.float32)
            grad = part if grad is None else grad + part
        out_ref[at, :] = base_ref[at, :] + user_rate * grad


SMALL = pltpu.CompilerParams(vmem_limit_bytes=12 * 2**20)
IN_VMEM = pl.BlockSpec(memory_space=pltpu.VMEM)


def begin(plan, item_factors, blk, user_rows):
    rows, rank = item_factors.shape
    in_smem = pl.BlockSpec(memory_space=pltpu.SMEM)

    def body(*refs):
        start_kernel(plan.shape[0], blk, *refs)

    return pl.pallas_call(
        body,
        out_shape=[
            jax.ShapeDtypeStruct((1,), jnp.int32),
            jax.ShapeDtypeStruct((2,), jnp.int32),
            jax.ShapeDtypeStruct((TWINS * rows, rank), jnp.float32),
            jax.ShapeDtypeStruct((user_rows, rank), jnp.float32),
        ],
        in_specs=[in_smem, IN_VMEM],
        out_specs=[in_smem, in_smem, IN_VMEM, pl.BlockSpec(memory_space=pl.ANY)],
        compiler_params=SMALL,
        name="begin",
    )(plan, item_factors)


def prepare(at, observed, ratings, start, held, user_noise, item_noise, rows, user_rate):
    user_rows, rank = start.shape
    items = ratings.shape[2]
    tile = pl.BlockSpec((1, CHUNK, items), lambda i, at: (at[0], i, 0))

    def body(*refs):
        prepare_kernel(user_rate, *refs)

    return pl.pallas_call(
        body,
        out_shape=[
            jax.ShapeDtypeStruct((user_rows, items), jnp.bfloat16),
            jax.ShapeDtypeStruct((user_rows, rank), jnp.float32),
            jax.ShapeDtypeStruct((user_rows, rank), jnp.bfloat16),
            jax.ShapeDtypeStruct((rank, user_rows), jnp.bfloat16),
            jax.ShapeDtypeStruct((rows, rank), jnp.float32),
        ],
        grid_spec=pltpu.PrefetchScalarGridSpec(
            num_scalar_prefetch=1,
            grid=(user_rows // CHUNK,),
            in_specs=[
                tile,
                tile,
                pl.BlockSpec((CHUNK, rank), lambda i, at: (i, 0)),
                pl.BlockSpec((CHUNK, rank), lambda i, at: (i, 0)),
                pl.BlockSpec((1, CHUNK, rank), lambda i, at: (at[0], i, 0)),
                pl.BlockSpec((1, rows, rank), lambda i, at: (at[0], at[1], 0)),
            ],
            out_specs=[IN_VMEM] * 5,
        ),
        compiler_params=SMALL,
        name="prepare",
    )(at, observed, ratings, start, held, user_noise, item_noise)


def piece_errors(back, piece, half, turned, coded):
    user_rows = half.shape[0]
    rows, rank = piece.shape

    def body(*refs):
        errors_kernel(back, *refs)

    return pl.pallas_call(
        body,
        out_shape=[
            jax.ShapeDtypeStruct((user_rows, rows), jnp.bfloat16),
            jax.ShapeDtypeStruct((rows, rank), jnp.float32),
        ],
        in_specs=[IN_VMEM] * 4,
        out_specs=[IN_VMEM] * 2,
        compiler_params=SMALL,
        name=f"errors{back}",
    )(piece, half, turned, coded)


def users_update(pieces, errors, base, user_rate):
    ring = len(pieces)

    def body(*refs):
        users_kernel(user_rate, ring, *refs)

    return pl.pallas_call(
        body,
        out_shape=jax.ShapeDtypeStruct(base.shape, jnp.float32),
        in_specs=[IN_VMEM] * (2 * ring + 1),
        out_specs=IN_VMEM,
        compiler_params=SMALL,
        name="users",
    )(*pieces, *errors, base)


def local(user_factors, item_factors, ratings, observed, plan, user_noise, item_noise):
    blk, shard = lax.axis_size("blk"), lax.axis_size("shard")
    ring = shard // TWINS
    user_rows = user_factors.shape[0]
    piece_rows = item_factors.shape[0]
    rows = piece_rows * TWINS
    user_rate = user_scale / ratings.shape[2]
    item_rate = item_scale / (shard * user_rows)
    twin = lax.axis_index("shard") % TWINS
    bits = (blk - 1).bit_length()

    code, at, share, room = begin(plan, item_factors, blk, user_rows)

    def one(at, users, share):
        flipped = moved(share, blk)
        ready = prepare(
            at, observed, ratings, user_factors, users, user_noise, item_noise, rows, user_rate
        )
        flipped, ready = lax.optimization_barrier((flipped, ready))
        coded, base, users_half, turned, noise = ready
        items = share + flipped
        half = items.astype(jnp.bfloat16)
        order = sorted(range(1, ring), key=lambda k: min(k, ring - k))
        away = {k: moved(half, 0, k) for k in order}
        kept = jnp.where(twin == 0, items - item_rate * prior * items + noise, 0.0)
        error, total = piece_errors(0, half, users_half, turned, coded)
        pieces, errors = [half], [error]
        for k in order:
            error, grad = piece_errors(k, away[k], users_half, turned, coded)
            pieces.append(away[k])
            errors.append(error)
            total = total + moved(grad, 0, -k)
        users = users_update(pieces, errors, base, user_rate)
        return users, kept + item_rate * total

    def none(at, users, share):
        return users, share + moved(share, blk)

    def trip(carry):
        code, at, users, share = carry
        share = rotated(share, code & ((1 << bits) - 1))
        code = code >> bits
        users, share = lax.cond(code > 1, one, none, at, users, share)
        return code, at + jnp.array([1, 0], jnp.int32), users, share

    held = (code[0], at, room, share)
    _, _, users, items = lax.while_loop(lambda carry: carry[0] > 1, trip, held)
    piece = lax.dynamic_slice_in_dim(items, twin * piece_rows, piece_rows, 0)
    return users, piece


def solution(mesh):
    in_specs = (
        P(("blk", "shard"), None),
        P(("blk", "shard"), None),
        P(None, ("blk", "shard"), None),
        P(None, ("blk", "shard"), None),
        P(),
        P(None, ("blk", "shard"), None),
        P(None, "blk", None),
    )
    out_specs = (P(("blk", "shard"), None), P(("blk", "shard"), None))
    return jax.shard_map(local, mesh=mesh, in_specs=in_specs, out_specs=out_specs, check_vma=False)
```

```python
import jax
import jax.numpy as jnp
from jax import lax
from jax.experimental import pallas as pl
from jax.experimental.pallas import tpu as pltpu
from jax.sharding import PartitionSpec as P


user_scale = 12.0
item_scale = 30.0
prior = 1.0

FLAT = ("blk", "shard")
TWINS = 2
CHUNK = 256
UNSEEN = 2.0**20


def pairs(blk, shard, distance, x_step):
    ring = shard // TWINS
    out = []
    for b in range(blk):
        for s in range(shard):
            x, twin = s // TWINS, s % TWINS
            far = (twin * blk + b + distance) % (TWINS * blk)
            to = ((x + x_step) % ring) * TWINS + far // blk
            out.append((b * shard + s, (far % blk) * shard + to))
    return out


def moved(value, distance, x_step=0):
    blk, shard = lax.axis_size("blk"), lax.axis_size("shard")
    if distance % (TWINS * blk) == 0 and x_step == 0:
        return value
    return lax.ppermute(value, FLAT, pairs(blk, shard, distance, x_step))


def rotated(share, steps):
    blk = lax.axis_size("blk")

    def branch(d):
        return lambda v: moved(v, d)

    return lax.switch(steps, [branch(d if d < blk // 2 else d - blk) for d in range(blk)], share)


def start_kernel(strata, blk, plan_ref, items_ref, *refs):
    steps, (share_ref, held_ref, sem, plan_sem) = refs[: strata + 1], refs[strata + 1 :]
    plan_copy = pltpu.make_async_copy(plan_ref, held_ref, plan_sem)
    plan_copy.start()
    rows = items_ref.shape[0]
    twin = lax.rem(lax.axis_index("shard"), TWINS)
    mine = pl.ds(pl.multiple_of(twin * rows, rows), rows)
    share_ref[...] = jnp.zeros_like(share_ref)
    copy = pltpu.make_async_copy(items_ref, share_ref.at[mine, :], sem)
    copy.start()
    plan_copy.wait()
    taken = 0
    for t in range(strata):
        steps[t][0] = held_ref[t]
        taken = taken + held_ref[t]
    steps[strata][0] = lax.rem(strata * blk - taken, blk)
    copy.wait()


def prepare_kernel(
    at_ref, observed_ref, ratings_ref, start_ref, held_ref, coded_ref, users_ref, half_ref, turned_ref
):
    step = pl.program_id(0)
    rows = pl.ds(pl.multiple_of(step * CHUNK, CHUNK), CHUNK)
    ratings = ratings_ref[0].astype(jnp.float32)
    coded_ref[rows, :] = jnp.where(observed_ref[0] != 0, ratings, UNSEEN).astype(jnp.bfloat16)

    @pl.when(at_ref[0] == 0)
    def _():
        users_ref[rows, :] = start_ref[...]

    @pl.when(at_ref[0] != 0)
    def _():
        users_ref[rows, :] = held_ref[rows, :]

    half = users_ref[rows, :].astype(jnp.bfloat16)
    half_ref[rows, :] = half
    turned_ref[:, rows] = half.T


def errors_kernel(back, piece_ref, half_ref, turned_ref, coded_ref, errors_ref, grad_ref):
    rows = piece_ref.shape[0]
    ring = coded_ref.shape[1] // rows
    x = lax.axis_index("shard") // TWINS
    place = pl.multiple_of(lax.rem(x + ring - back, ring) * rows, rows)
    piece = piece_ref[...]
    for c in range(half_ref.shape[0] // CHUNK):
        at = pl.ds(c * CHUNK, CHUNK)
        predicted = lax.dot_general(
            half_ref[at, :], piece, (((1,), (1,)), ((), ())), preferred_element_type=jnp.float32
        )
        coded = coded_ref[at, pl.ds(place, rows)].astype(jnp.float32)
        errors = jnp.where(coded < 0.5 * UNSEEN, coded - predicted, 0.0)
        errors_ref[at, :] = errors.astype(jnp.bfloat16)
    grad = jnp.dot(turned_ref[...], errors_ref[...], preferred_element_type=jnp.float32)
    grad_ref[...] = grad.T


def users_kernel(user_rate, ring, *refs):
    pieces, errors, (users_ref, noise_ref, out_ref) = refs[:ring], refs[ring : 2 * ring], refs[2 * ring :]
    for c in range(users_ref.shape[0] // CHUNK):
        at = pl.ds(c * CHUNK, CHUNK)
        users = users_ref[at, :]
        grad = None
        for piece, error in zip(pieces, errors):
            part = jnp.dot(error[at, :], piece[...], preferred_element_type=jnp.float32)
            grad = part if grad is None else grad + part
        out_ref[at, :] = users + user_rate * (grad - prior * users) + noise_ref[at, :]


SMALL = pltpu.CompilerParams(vmem_limit_bytes=12 * 2**20)
IN_VMEM = pl.BlockSpec(memory_space=pltpu.VMEM)


def begin(plan, item_factors, blk):
    strata = plan.shape[0]
    rows, rank = item_factors.shape
    in_smem = pl.BlockSpec(memory_space=pltpu.SMEM)

    def body(*refs):
        start_kernel(strata, blk, *refs)

    out = pl.pallas_call(
        body,
        out_shape=[jax.ShapeDtypeStruct((1,), jnp.int32)] * (strata + 1)
        + [jax.ShapeDtypeStruct((TWINS * rows, rank), jnp.float32)],
        in_specs=[pl.BlockSpec(memory_space=pltpu.HBM)] * 2,
        out_specs=[in_smem] * (strata + 1) + [IN_VMEM],
        scratch_shapes=[pltpu.SMEM((strata,), jnp.int32)] + [pltpu.SemaphoreType.DMA] * 2,
        compiler_params=SMALL,
        name="begin",
    )(
        pltpu.with_memory_space_constraint(plan, pltpu.HBM),
        pltpu.with_memory_space_constraint(item_factors, pltpu.HBM),
    )
    return [step[0] for step in out[:-1]], out[-1]


def prepare(at, observed, ratings, start, held):
    user_rows, rank = start.shape
    items = ratings.shape[2]
    tile = pl.BlockSpec((1, CHUNK, items), lambda i, at: (at[0], i, 0))
    return pl.pallas_call(
        prepare_kernel,
        out_shape=[
            jax.ShapeDtypeStruct((user_rows, items), jnp.bfloat16),
            jax.ShapeDtypeStruct((user_rows, rank), jnp.float32),
            jax.ShapeDtypeStruct((user_rows, rank), jnp.bfloat16),
            jax.ShapeDtypeStruct((rank, user_rows), jnp.bfloat16),
        ],
        grid_spec=pltpu.PrefetchScalarGridSpec(
            num_scalar_prefetch=1,
            grid=(user_rows // CHUNK,),
            in_specs=[tile, tile, pl.BlockSpec((CHUNK, rank), lambda i, at: (i, 0)), IN_VMEM],
            out_specs=[IN_VMEM] * 4,
        ),
        compiler_params=SMALL,
        name="prepare",
    )(at, observed, ratings, start, held)


def piece_errors(back, piece, half, turned, coded):
    user_rows = half.shape[0]
    rows, rank = piece.shape

    def body(*refs):
        errors_kernel(back, *refs)

    return pl.pallas_call(
        body,
        out_shape=[
            jax.ShapeDtypeStruct((user_rows, rows), jnp.bfloat16),
            jax.ShapeDtypeStruct((rows, rank), jnp.float32),
        ],
        in_specs=[IN_VMEM] * 4,
        out_specs=[IN_VMEM] * 2,
        compiler_params=SMALL,
        name=f"errors{back}",
    )(piece, half, turned, coded)


def users_update(pieces, errors, users, noise, user_rate):
    ring = len(pieces)

    def body(*refs):
        users_kernel(user_rate, ring, *refs)

    return pl.pallas_call(
        body,
        out_shape=jax.ShapeDtypeStruct(users.shape, jnp.float32),
        in_specs=[IN_VMEM] * (2 * ring + 2),
        out_specs=IN_VMEM,
        compiler_params=SMALL,
        name="users",
    )(*pieces, *errors, users, noise)


def local(user_factors, item_factors, ratings, observed, plan, user_noise, item_noise):
    blk, shard = lax.axis_size("blk"), lax.axis_size("shard")
    ring = shard // TWINS
    user_rows = user_factors.shape[0]
    piece_rows = item_factors.shape[0]
    rows = piece_rows * TWINS
    user_rate = user_scale / ratings.shape[2]
    item_rate = item_scale / (shard * user_rows)
    strata = ratings.shape[0]
    x = lax.axis_index("shard") // TWINS
    twin = lax.axis_index("shard") % TWINS

    steps, share = begin(plan, item_factors, blk)

    def one(t, users, share):
        at = jnp.stack([t, x]).astype(jnp.int32)
        noise = lax.dynamic_slice(item_noise, (t, x * rows, 0), (1, rows, item_noise.shape[2]))[0]
        flipped = moved(share, blk)
        ready = prepare(at, observed, ratings, user_factors, users)
        flipped, ready, noise = lax.optimization_barrier((flipped, ready, noise))
        coded, users, users_half, turned = ready
        items = share + flipped
        half = items.astype(jnp.bfloat16)
        order = sorted(range(1, ring), key=lambda k: min(k, ring - k))
        away = {k: moved(half, 0, k) for k in order}
        drift = lax.dynamic_index_in_dim(user_noise, t, keepdims=False)
        kept = jnp.where(twin == 0, items - item_rate * prior * items + noise, 0.0)
        error, total = piece_errors(0, half, users_half, turned, coded)
        pieces, errors = [half], [error]
        for k in order:
            error, grad = piece_errors(k, away[k], users_half, turned, coded)
            pieces.append(away[k])
            errors.append(error)
            total = total + moved(grad, 0, -k)
        users = users_update(pieces, errors, users, drift, user_rate)
        return users, kept + item_rate * total

    def none(t, users, share):
        mine = lax.dynamic_slice_in_dim(share, twin * piece_rows, piece_rows, 0)
        given = lax.dynamic_slice_in_dim(share, (1 - twin) * piece_rows, piece_rows, 0)
        piece = mine + moved(given, blk)
        return users, jnp.concatenate([piece, piece], 0)

    def trip(t, carry):
        users, share = carry
        step = steps[strata]
        for k in range(strata):
            step = jnp.where(t == k, steps[k], step)
        return lax.cond(t < strata, one, none, t, users, rotated(share, step))

    users, items = lax.fori_loop(0, strata + 1, trip, (jnp.zeros_like(user_factors), share))
    return users, items[:piece_rows]


def solution(mesh):
    in_specs = (
        P(("blk", "shard"), None),
        P(("blk", "shard"), None),
        P(None, ("blk", "shard"), None),
        P(None, ("blk", "shard"), None),
        P(),
        P(None, ("blk", "shard"), None),
        P(None, "blk", None),
    )
    out_specs = (P(("blk", "shard"), None), P(("blk", "shard"), None))
    return jax.shard_map(local, mesh=mesh, in_specs=in_specs, out_specs=out_specs, check_vma=False)
```

```python
import jax
import jax.numpy as jnp
from jax import lax
from jax.experimental import pallas as pl
from jax.experimental.pallas import tpu as pltpu
from jax.sharding import PartitionSpec as P


user_scale = 12.0
item_scale = 30.0
prior = 1.0

FLAT = ("blk", "shard")
TWINS = 2
CHUNK = 256
UNSEEN = 2.0**20


def pairs(blk, shard, distance, x_step):
    ring = shard // TWINS
    out = []
    for b in range(blk):
        for s in range(shard):
            x, twin = s // TWINS, s % TWINS
            far = (twin * blk + b + distance) % (TWINS * blk)
            to = ((x + x_step) % ring) * TWINS + far // blk
            out.append((b * shard + s, (far % blk) * shard + to))
    return out


def moved(value, distance, x_step=0):
    blk, shard = lax.axis_size("blk"), lax.axis_size("shard")
    if distance % (TWINS * blk) == 0 and x_step == 0:
        return value
    return lax.ppermute(value, FLAT, pairs(blk, shard, distance, x_step))


def rotated(share, steps):
    blk = lax.axis_size("blk")

    def branch(d):
        return lambda v: moved(v, d)

    return lax.switch(steps, [branch(d if d < blk // 2 else d - blk) for d in range(blk)], share)


def start_kernel(strata, blk, plan_ref, items_ref, *refs):
    code_ref, share_ref, held_ref, sem, plan_sem = refs
    bits = (blk - 1).bit_length()
    plan_copy = pltpu.make_async_copy(plan_ref, held_ref, plan_sem)
    plan_copy.start()
    rows = items_ref.shape[0]
    twin = lax.rem(lax.axis_index("shard"), TWINS)
    mine = pl.ds(pl.multiple_of(twin * rows, rows), rows)
    share_ref[...] = jnp.zeros_like(share_ref)
    copy = pltpu.make_async_copy(items_ref, share_ref.at[mine, :], sem)
    copy.start()
    plan_copy.wait()
    code, taken = 0, 0
    for t in range(strata):
        code = code + held_ref[t] * (1 << (t * bits))
        taken = taken + held_ref[t]
    code_ref[0] = code + lax.rem(strata * blk - taken, blk) * (1 << (strata * bits))
    copy.wait()


def prepare_kernel(
    at_ref, observed_ref, ratings_ref, start_ref, held_ref, coded_ref, users_ref, half_ref, turned_ref
):
    step = pl.program_id(0)
    rows = pl.ds(pl.multiple_of(step * CHUNK, CHUNK), CHUNK)
    ratings = ratings_ref[0].astype(jnp.float32)
    coded_ref[rows, :] = jnp.where(observed_ref[0] != 0, ratings, UNSEEN).astype(jnp.bfloat16)

    @pl.when(at_ref[0] == 0)
    def _():
        users_ref[rows, :] = start_ref[...]

    @pl.when(at_ref[0] != 0)
    def _():
        users_ref[rows, :] = held_ref[rows, :]

    half = users_ref[rows, :].astype(jnp.bfloat16)
    half_ref[rows, :] = half
    turned_ref[:, rows] = half.T


def errors_kernel(back, piece_ref, half_ref, turned_ref, coded_ref, errors_ref, grad_ref):
    rows = piece_ref.shape[0]
    ring = coded_ref.shape[1] // rows
    x = lax.axis_index("shard") // TWINS
    place = pl.multiple_of(lax.rem(x + ring - back, ring) * rows, rows)
    piece = piece_ref[...]
    for c in range(half_ref.shape[0] // CHUNK):
        at = pl.ds(c * CHUNK, CHUNK)
        predicted = lax.dot_general(
            half_ref[at, :], piece, (((1,), (1,)), ((), ())), preferred_element_type=jnp.float32
        )
        coded = coded_ref[at, pl.ds(place, rows)].astype(jnp.float32)
        errors = jnp.where(coded < 0.5 * UNSEEN, coded - predicted, 0.0)
        errors_ref[at, :] = errors.astype(jnp.bfloat16)
    grad = jnp.dot(turned_ref[...], errors_ref[...], preferred_element_type=jnp.float32)
    grad_ref[...] = grad.T


def users_kernel(user_rate, ring, *refs):
    pieces, errors, (users_ref, noise_ref, out_ref) = refs[:ring], refs[ring : 2 * ring], refs[2 * ring :]
    for c in range(users_ref.shape[0] // CHUNK):
        at = pl.ds(c * CHUNK, CHUNK)
        users = users_ref[at, :]
        grad = None
        for piece, error in zip(pieces, errors):
            part = jnp.dot(error[at, :], piece[...], preferred_element_type=jnp.float32)
            grad = part if grad is None else grad + part
        out_ref[at, :] = users + user_rate * (grad - prior * users) + noise_ref[at, :]


SMALL = pltpu.CompilerParams(vmem_limit_bytes=12 * 2**20)
IN_VMEM = pl.BlockSpec(memory_space=pltpu.VMEM)


def begin(plan, item_factors, blk):
    strata = plan.shape[0]
    rows, rank = item_factors.shape
    in_smem = pl.BlockSpec(memory_space=pltpu.SMEM)

    def body(*refs):
        start_kernel(strata, blk, *refs)

    code, share = pl.pallas_call(
        body,
        out_shape=[
            jax.ShapeDtypeStruct((1,), jnp.int32),
            jax.ShapeDtypeStruct((TWINS * rows, rank), jnp.float32),
        ],
        in_specs=[pl.BlockSpec(memory_space=pltpu.HBM)] * 2,
        out_specs=[in_smem, IN_VMEM],
        scratch_shapes=[pltpu.SMEM((strata,), jnp.int32)] + [pltpu.SemaphoreType.DMA] * 2,
        compiler_params=SMALL,
        name="begin",
    )(
        pltpu.with_memory_space_constraint(plan, pltpu.HBM),
        pltpu.with_memory_space_constraint(item_factors, pltpu.HBM),
    )
    return code[0], share


def prepare(at, observed, ratings, start, held):
    user_rows, rank = start.shape
    items = ratings.shape[2]
    tile = pl.BlockSpec((1, CHUNK, items), lambda i, at: (at[0], i, 0))
    return pl.pallas_call(
        prepare_kernel,
        out_shape=[
            jax.ShapeDtypeStruct((user_rows, items), jnp.bfloat16),
            jax.ShapeDtypeStruct((user_rows, rank), jnp.float32),
            jax.ShapeDtypeStruct((user_rows, rank), jnp.bfloat16),
            jax.ShapeDtypeStruct((rank, user_rows), jnp.bfloat16),
        ],
        grid_spec=pltpu.PrefetchScalarGridSpec(
            num_scalar_prefetch=1,
            grid=(user_rows // CHUNK,),
            in_specs=[tile, tile, pl.BlockSpec((CHUNK, rank), lambda i, at: (i, 0)), IN_VMEM],
            out_specs=[IN_VMEM] * 4,
        ),
        compiler_params=SMALL,
        name="prepare",
    )(at, observed, ratings, start, held)


def piece_errors(back, piece, half, turned, coded):
    user_rows = half.shape[0]
    rows, rank = piece.shape

    def body(*refs):
        errors_kernel(back, *refs)

    return pl.pallas_call(
        body,
        out_shape=[
            jax.ShapeDtypeStruct((user_rows, rows), jnp.bfloat16),
            jax.ShapeDtypeStruct((rows, rank), jnp.float32),
        ],
        in_specs=[IN_VMEM] * 4,
        out_specs=[IN_VMEM] * 2,
        compiler_params=SMALL,
        name=f"errors{back}",
    )(piece, half, turned, coded)


def users_update(pieces, errors, users, noise, user_rate):
    ring = len(pieces)

    def body(*refs):
        users_kernel(user_rate, ring, *refs)

    return pl.pallas_call(
        body,
        out_shape=jax.ShapeDtypeStruct(users.shape, jnp.float32),
        in_specs=[IN_VMEM] * (2 * ring + 2),
        out_specs=IN_VMEM,
        compiler_params=SMALL,
        name="users",
    )(*pieces, *errors, users, noise)


def local(user_factors, item_factors, ratings, observed, plan, user_noise, item_noise):
    blk, shard = lax.axis_size("blk"), lax.axis_size("shard")
    ring = shard // TWINS
    user_rows = user_factors.shape[0]
    piece_rows = item_factors.shape[0]
    rows = piece_rows * TWINS
    user_rate = user_scale / ratings.shape[2]
    item_rate = item_scale / (shard * user_rows)
    strata = ratings.shape[0]
    x = lax.axis_index("shard") // TWINS
    twin = lax.axis_index("shard") % TWINS

    code, share = begin(plan, item_factors, blk)
    bits = (blk - 1).bit_length()

    def one(t, users, share):
        at = jnp.stack([t, x]).astype(jnp.int32)
        noise = lax.dynamic_slice(item_noise, (t, x * rows, 0), (1, rows, item_noise.shape[2]))[0]
        flipped = moved(share, blk)
        ready = prepare(at, observed, ratings, user_factors, users)
        flipped, ready, noise = lax.optimization_barrier((flipped, ready, noise))
        coded, users, users_half, turned = ready
        items = share + flipped
        half = items.astype(jnp.bfloat16)
        order = sorted(range(1, ring), key=lambda k: min(k, ring - k))
        away = {k: moved(half, 0, k) for k in order}
        drift = lax.dynamic_index_in_dim(user_noise, t, keepdims=False)
        kept = jnp.where(twin == 0, items - item_rate * prior * items + noise, 0.0)
        error, total = piece_errors(0, half, users_half, turned, coded)
        pieces, errors = [half], [error]
        for k in order:
            error, grad = piece_errors(k, away[k], users_half, turned, coded)
            pieces.append(away[k])
            errors.append(error)
            total = total + moved(grad, 0, -k)
        users = users_update(pieces, errors, users, drift, user_rate)
        return users, kept + item_rate * total

    def none(t, users, share):
        mine = lax.dynamic_slice_in_dim(share, twin * piece_rows, piece_rows, 0)
        given = lax.dynamic_slice_in_dim(share, (1 - twin) * piece_rows, piece_rows, 0)
        piece = mine + moved(given, blk)
        return users, jnp.concatenate([piece, piece], 0)

    def trip(t, carry):
        users, share = carry
        step = (code >> (t * bits)) & ((1 << bits) - 1)
        return lax.cond(t < strata, one, none, t, users, rotated(share, step))

    users, items = lax.fori_loop(0, strata + 1, trip, (jnp.zeros_like(user_factors), share))
    return users, items[:piece_rows]


def solution(mesh):
    in_specs = (
        P(("blk", "shard"), None),
        P(("blk", "shard"), None),
        P(None, ("blk", "shard"), None),
        P(None, ("blk", "shard"), None),
        P(),
        P(None, ("blk", "shard"), None),
        P(None, "blk", None),
    )
    out_specs = (P(("blk", "shard"), None), P(("blk", "shard"), None))
    return jax.shard_map(local, mesh=mesh, in_specs=in_specs, out_specs=out_specs, check_vma=False)
```

```python
import jax
import jax.numpy as jnp
from jax import lax
from jax.experimental import pallas as pl
from jax.experimental.pallas import tpu as pltpu
from jax.sharding import PartitionSpec as P


user_scale = 12.0
item_scale = 30.0
prior = 1.0

FLAT = ("blk", "shard")
TWINS = 2
CHUNK = 256
UNSEEN = 2.0**20


def pairs(blk, shard, distance, x_step):
    ring = shard // TWINS
    out = []
    for b in range(blk):
        for s in range(shard):
            x, twin = s // TWINS, s % TWINS
            far = (twin * blk + b + distance) % (TWINS * blk)
            to = ((x + x_step) % ring) * TWINS + far // blk
            out.append((b * shard + s, (far % blk) * shard + to))
    return out


def moved(value, distance, x_step=0):
    blk, shard = lax.axis_size("blk"), lax.axis_size("shard")
    if distance % (TWINS * blk) == 0 and x_step == 0:
        return value
    return lax.ppermute(value, FLAT, pairs(blk, shard, distance, x_step))


def rotated(share, steps):
    blk = lax.axis_size("blk")

    def branch(d):
        return lambda v: moved(v, d)

    return lax.switch(steps, [branch(d if d < blk // 2 else d - blk) for d in range(blk)], share)


def start_kernel(strata, blk, plan_ref, items_ref, *refs):
    code_ref, share_ref, held_ref, sem, plan_sem = refs
    bits = (blk - 1).bit_length()
    plan_copy = pltpu.make_async_copy(plan_ref, held_ref, plan_sem)
    plan_copy.start()
    rows = items_ref.shape[0]
    twin = lax.rem(lax.axis_index("shard"), TWINS)
    mine = pl.ds(pl.multiple_of(twin * rows, rows), rows)
    share_ref[...] = jnp.zeros_like(share_ref)
    copy = pltpu.make_async_copy(items_ref, share_ref.at[mine, :], sem)
    copy.start()
    plan_copy.wait()
    code, taken = 0, 0
    for t in range(strata):
        code = code + held_ref[t] * (1 << (t * bits))
        taken = taken + held_ref[t]
    code_ref[0] = code + lax.rem(strata * blk - taken, blk) * (1 << (strata * bits))
    copy.wait()


def prepare_kernel(
    at_ref, observed_ref, ratings_ref, start_ref, held_ref, coded_ref, users_ref, half_ref, turned_ref
):
    step = pl.program_id(0)
    rows = pl.ds(pl.multiple_of(step * CHUNK, CHUNK), CHUNK)
    ratings = ratings_ref[0].astype(jnp.float32)
    coded_ref[rows, :] = jnp.where(observed_ref[0] != 0, ratings, UNSEEN).astype(jnp.bfloat16)

    @pl.when(at_ref[0] == 0)
    def _():
        users_ref[rows, :] = start_ref[...]

    @pl.when(at_ref[0] != 0)
    def _():
        users_ref[rows, :] = held_ref[rows, :]

    half = users_ref[rows, :].astype(jnp.bfloat16)
    half_ref[rows, :] = half
    turned_ref[:, rows] = half.T


def errors_kernel(back, piece_ref, half_ref, turned_ref, coded_ref, errors_ref, grad_ref):
    rows = piece_ref.shape[0]
    ring = coded_ref.shape[1] // rows
    x = lax.axis_index("shard") // TWINS
    place = pl.multiple_of(lax.rem(x + ring - back, ring) * rows, rows)
    piece = piece_ref[...]
    for c in range(half_ref.shape[0] // CHUNK):
        at = pl.ds(c * CHUNK, CHUNK)
        predicted = lax.dot_general(
            half_ref[at, :], piece, (((1,), (1,)), ((), ())), preferred_element_type=jnp.float32
        )
        coded = coded_ref[at, pl.ds(place, rows)].astype(jnp.float32)
        errors = jnp.where(coded < 0.5 * UNSEEN, coded - predicted, 0.0)
        errors_ref[at, :] = errors.astype(jnp.bfloat16)
    grad = jnp.dot(turned_ref[...], errors_ref[...], preferred_element_type=jnp.float32)
    grad_ref[...] = grad.T


def users_kernel(user_rate, ring, *refs):
    pieces, errors, (users_ref, noise_ref, out_ref) = refs[:ring], refs[ring : 2 * ring], refs[2 * ring :]
    for c in range(users_ref.shape[0] // CHUNK):
        at = pl.ds(c * CHUNK, CHUNK)
        users = users_ref[at, :]
        grad = None
        for piece, error in zip(pieces, errors):
            part = jnp.dot(error[at, :], piece[...], preferred_element_type=jnp.float32)
            grad = part if grad is None else grad + part
        out_ref[at, :] = users + user_rate * (grad - prior * users) + noise_ref[at, :]


SMALL = pltpu.CompilerParams(vmem_limit_bytes=12 * 2**20)
IN_VMEM = pl.BlockSpec(memory_space=pltpu.VMEM)


def begin(plan, item_factors, blk):
    strata = plan.shape[0]
    rows, rank = item_factors.shape
    in_smem = pl.BlockSpec(memory_space=pltpu.SMEM)

    def body(*refs):
        start_kernel(strata, blk, *refs)

    code, share = pl.pallas_call(
        body,
        out_shape=[
            jax.ShapeDtypeStruct((1,), jnp.int32),
            jax.ShapeDtypeStruct((TWINS * rows, rank), jnp.float32),
        ],
        in_specs=[pl.BlockSpec(memory_space=pltpu.HBM)] * 2,
        out_specs=[in_smem, IN_VMEM],
        scratch_shapes=[pltpu.SMEM((strata,), jnp.int32)] + [pltpu.SemaphoreType.DMA] * 2,
        compiler_params=SMALL,
        name="begin",
    )(
        pltpu.with_memory_space_constraint(plan, pltpu.HBM),
        pltpu.with_memory_space_constraint(item_factors, pltpu.HBM),
    )
    return code[0], share


def prepare(at, observed, ratings, start, held):
    user_rows, rank = start.shape
    items = ratings.shape[2]
    tile = pl.BlockSpec((1, CHUNK, items), lambda i, at: (at[0], i, 0))
    return pl.pallas_call(
        prepare_kernel,
        out_shape=[
            jax.ShapeDtypeStruct((user_rows, items), jnp.bfloat16),
            jax.ShapeDtypeStruct((user_rows, rank), jnp.float32),
            jax.ShapeDtypeStruct((user_rows, rank), jnp.bfloat16),
            jax.ShapeDtypeStruct((rank, user_rows), jnp.bfloat16),
        ],
        grid_spec=pltpu.PrefetchScalarGridSpec(
            num_scalar_prefetch=1,
            grid=(user_rows // CHUNK,),
            in_specs=[tile, tile, pl.BlockSpec((CHUNK, rank), lambda i, at: (i, 0)), IN_VMEM],
            out_specs=[IN_VMEM] * 4,
        ),
        compiler_params=SMALL,
        name="prepare",
    )(at, observed, ratings, start, held)


def piece_errors(back, piece, half, turned, coded):
    user_rows = half.shape[0]
    rows, rank = piece.shape

    def body(*refs):
        errors_kernel(back, *refs)

    return pl.pallas_call(
        body,
        out_shape=[
            jax.ShapeDtypeStruct((user_rows, rows), jnp.bfloat16),
            jax.ShapeDtypeStruct((rows, rank), jnp.float32),
        ],
        in_specs=[IN_VMEM] * 4,
        out_specs=[IN_VMEM] * 2,
        compiler_params=SMALL,
        name=f"errors{back}",
    )(piece, half, turned, coded)


def users_update(pieces, errors, users, noise, user_rate):
    ring = len(pieces)

    def body(*refs):
        users_kernel(user_rate, ring, *refs)

    return pl.pallas_call(
        body,
        out_shape=jax.ShapeDtypeStruct(users.shape, jnp.float32),
        in_specs=[IN_VMEM] * (2 * ring + 2),
        out_specs=IN_VMEM,
        compiler_params=SMALL,
        name="users",
    )(*pieces, *errors, users, noise)


def local(user_factors, item_factors, ratings, observed, plan, user_noise, item_noise):
    blk, shard = lax.axis_size("blk"), lax.axis_size("shard")
    ring = shard // TWINS
    user_rows = user_factors.shape[0]
    piece_rows = item_factors.shape[0]
    rows = piece_rows * TWINS
    user_rate = user_scale / ratings.shape[2]
    item_rate = item_scale / (shard * user_rows)
    strata = ratings.shape[0]
    x = lax.axis_index("shard") // TWINS
    twin = lax.axis_index("shard") % TWINS

    code, share = begin(plan, item_factors, blk)
    bits = (blk - 1).bit_length()

    def one(t, users, share):
        at = jnp.stack([t, x]).astype(jnp.int32)
        noise = lax.dynamic_slice(item_noise, (t, x * rows, 0), (1, rows, item_noise.shape[2]))[0]
        flipped = moved(share, blk)
        ready = prepare(at, observed, ratings, user_factors, users)
        flipped, ready, noise = lax.optimization_barrier((flipped, ready, noise))
        coded, users, users_half, turned = ready
        items = share + flipped
        half = items.astype(jnp.bfloat16)
        order = sorted(range(1, ring), key=lambda k: min(k, ring - k))
        away = {k: moved(half, 0, k) for k in order}
        drift = lax.dynamic_index_in_dim(user_noise, t, keepdims=False)
        kept = jnp.where(twin == 0, items - item_rate * prior * items + noise, 0.0)
        error, total = piece_errors(0, half, users_half, turned, coded)
        half, total, coded = lax.optimization_barrier((half, total, coded))
        pieces, errors = [half], [error]
        for k in order:
            error, grad = piece_errors(k, away[k], users_half, turned, coded)
            pieces.append(away[k])
            errors.append(error)
            total = total + moved(grad, 0, -k)
        users = users_update(pieces, errors, users, drift, user_rate)
        return users, kept + item_rate * total

    def none(t, users, share):
        mine = lax.dynamic_slice_in_dim(share, twin * piece_rows, piece_rows, 0)
        given = lax.dynamic_slice_in_dim(share, (1 - twin) * piece_rows, piece_rows, 0)
        piece = mine + moved(given, blk)
        return users, jnp.concatenate([piece, piece], 0)

    def trip(t, carry):
        users, share = carry
        step = (code >> (t * bits)) & ((1 << bits) - 1)
        return lax.cond(t < strata, one, none, t, users, rotated(share, step))

    users, items = lax.fori_loop(0, strata + 1, trip, (jnp.zeros_like(user_factors), share))
    return users, items[:piece_rows]


def solution(mesh):
    in_specs = (
        P(("blk", "shard"), None),
        P(("blk", "shard"), None),
        P(None, ("blk", "shard"), None),
        P(None, ("blk", "shard"), None),
        P(),
        P(None, ("blk", "shard"), None),
        P(None, "blk", None),
    )
    out_specs = (P(("blk", "shard"), None), P(("blk", "shard"), None))
    return jax.shard_map(local, mesh=mesh, in_specs=in_specs, out_specs=out_specs, check_vma=False)
```

```python
import jax
import jax.numpy as jnp
from jax import lax
from jax.experimental import pallas as pl
from jax.experimental.pallas import tpu as pltpu
from jax.sharding import PartitionSpec as P


user_scale = 12.0
item_scale = 30.0
prior = 1.0

FLAT = ("blk", "shard")
TWINS = 2
CHUNK = 256
UNSEEN = 2.0**20


def pairs(blk, shard, distance, x_step):
    ring = shard // TWINS
    out = []
    for b in range(blk):
        for s in range(shard):
            x, twin = s // TWINS, s % TWINS
            far = (twin * blk + b + distance) % (TWINS * blk)
            to = ((x + x_step) % ring) * TWINS + far // blk
            out.append((b * shard + s, (far % blk) * shard + to))
    return out


def moved(value, distance, x_step=0):
    blk, shard = lax.axis_size("blk"), lax.axis_size("shard")
    if distance % (TWINS * blk) == 0 and x_step == 0:
        return value
    return lax.ppermute(value, FLAT, pairs(blk, shard, distance, x_step))


def rotated(share, steps):
    blk = lax.axis_size("blk")

    def branch(d):
        return lambda v: moved(v, d)

    return lax.switch(steps, [branch(d if d < blk // 2 else d - blk) for d in range(blk)], share)


def start_kernel(strata, blk, plan_ref, items_ref, *refs):
    code_ref, share_ref, held_ref, sem, plan_sem = refs
    bits = (blk - 1).bit_length()
    plan_copy = pltpu.make_async_copy(plan_ref, held_ref, plan_sem)
    plan_copy.start()
    rows = items_ref.shape[0]
    twin = lax.rem(lax.axis_index("shard"), TWINS)
    mine = pl.ds(pl.multiple_of(twin * rows, rows), rows)
    share_ref[...] = jnp.zeros_like(share_ref)
    copy = pltpu.make_async_copy(items_ref, share_ref.at[mine, :], sem)
    copy.start()
    plan_copy.wait()
    code, taken = 0, 0
    for t in range(strata):
        code = code + held_ref[t] * (1 << (t * bits))
        taken = taken + held_ref[t]
    code_ref[0] = code + lax.rem(strata * blk - taken, blk) * (1 << (strata * bits))
    copy.wait()


def prepare_kernel(
    at_ref, observed_ref, ratings_ref, start_ref, held_ref, coded_ref, users_ref, half_ref, turned_ref
):
    step = pl.program_id(0)
    rows = pl.ds(pl.multiple_of(step * CHUNK, CHUNK), CHUNK)
    ratings = ratings_ref[0].astype(jnp.float32)
    coded_ref[rows, :] = jnp.where(observed_ref[0] != 0, ratings, UNSEEN).astype(jnp.bfloat16)

    @pl.when(at_ref[0] == 0)
    def _():
        users_ref[rows, :] = start_ref[...]

    @pl.when(at_ref[0] != 0)
    def _():
        users_ref[rows, :] = held_ref[rows, :]

    half = users_ref[rows, :].astype(jnp.bfloat16)
    half_ref[rows, :] = half
    turned_ref[:, rows] = half.T


def errors_kernel(back, piece_ref, half_ref, turned_ref, coded_ref, errors_ref, grad_ref):
    rows = piece_ref.shape[0]
    ring = coded_ref.shape[1] // rows
    x = lax.axis_index("shard") // TWINS
    place = pl.multiple_of(lax.rem(x + ring - back, ring) * rows, rows)
    piece = piece_ref[...]
    for c in range(half_ref.shape[0] // CHUNK):
        at = pl.ds(c * CHUNK, CHUNK)
        predicted = lax.dot_general(
            half_ref[at, :], piece, (((1,), (1,)), ((), ())), preferred_element_type=jnp.float32
        )
        coded = coded_ref[at, pl.ds(place, rows)].astype(jnp.float32)
        errors = jnp.where(coded < 0.5 * UNSEEN, coded - predicted, 0.0)
        errors_ref[at, :] = errors.astype(jnp.bfloat16)
    grad = jnp.dot(turned_ref[...], errors_ref[...], preferred_element_type=jnp.float32)
    grad_ref[...] = grad.T


def users_kernel(user_rate, ring, *refs):
    pieces, errors, (users_ref, noise_ref, out_ref) = refs[:ring], refs[ring : 2 * ring], refs[2 * ring :]
    for c in range(users_ref.shape[0] // CHUNK):
        at = pl.ds(c * CHUNK, CHUNK)
        users = users_ref[at, :]
        grad = None
        for piece, error in zip(pieces, errors):
            part = jnp.dot(error[at, :], piece[...], preferred_element_type=jnp.float32)
            grad = part if grad is None else grad + part
        out_ref[at, :] = users + user_rate * (grad - prior * users) + noise_ref[at, :]


SMALL = pltpu.CompilerParams(vmem_limit_bytes=12 * 2**20)
IN_VMEM = pl.BlockSpec(memory_space=pltpu.VMEM)


def begin(plan, item_factors, blk):
    strata = plan.shape[0]
    rows, rank = item_factors.shape
    in_smem = pl.BlockSpec(memory_space=pltpu.SMEM)

    def body(*refs):
        start_kernel(strata, blk, *refs)

    code, share = pl.pallas_call(
        body,
        out_shape=[
            jax.ShapeDtypeStruct((1,), jnp.int32),
            jax.ShapeDtypeStruct((TWINS * rows, rank), jnp.float32),
        ],
        in_specs=[pl.BlockSpec(memory_space=pltpu.HBM)] * 2,
        out_specs=[in_smem, IN_VMEM],
        scratch_shapes=[pltpu.SMEM((strata,), jnp.int32)] + [pltpu.SemaphoreType.DMA] * 2,
        compiler_params=SMALL,
        name="begin",
    )(
        pltpu.with_memory_space_constraint(plan, pltpu.HBM),
        pltpu.with_memory_space_constraint(item_factors, pltpu.HBM),
    )
    return code[0], share


def prepare(at, observed, ratings, start, held):
    user_rows, rank = start.shape
    items = ratings.shape[2]
    tile = pl.BlockSpec((1, CHUNK, items), lambda i, at: (at[0], i, 0))
    return pl.pallas_call(
        prepare_kernel,
        out_shape=[
            jax.ShapeDtypeStruct((user_rows, items), jnp.bfloat16),
            jax.ShapeDtypeStruct((user_rows, rank), jnp.float32),
            jax.ShapeDtypeStruct((user_rows, rank), jnp.bfloat16),
            jax.ShapeDtypeStruct((rank, user_rows), jnp.bfloat16),
        ],
        grid_spec=pltpu.PrefetchScalarGridSpec(
            num_scalar_prefetch=1,
            grid=(user_rows // CHUNK,),
            in_specs=[tile, tile, pl.BlockSpec((CHUNK, rank), lambda i, at: (i, 0)), IN_VMEM],
            out_specs=[IN_VMEM] * 4,
        ),
        compiler_params=SMALL,
        name="prepare",
    )(at, observed, ratings, start, held)


def piece_errors(back, piece, half, turned, coded):
    user_rows = half.shape[0]
    rows, rank = piece.shape

    def body(*refs):
        errors_kernel(back, *refs)

    return pl.pallas_call(
        body,
        out_shape=[
            jax.ShapeDtypeStruct((user_rows, rows), jnp.bfloat16),
            jax.ShapeDtypeStruct((rows, rank), jnp.float32),
        ],
        in_specs=[IN_VMEM] * 4,
        out_specs=[IN_VMEM] * 2,
        compiler_params=SMALL,
        name=f"errors{back}",
    )(piece, half, turned, coded)


def users_update(pieces, errors, users, noise, user_rate):
    ring = len(pieces)

    def body(*refs):
        users_kernel(user_rate, ring, *refs)

    return pl.pallas_call(
        body,
        out_shape=jax.ShapeDtypeStruct(users.shape, jnp.float32),
        in_specs=[IN_VMEM] * (2 * ring + 2),
        out_specs=IN_VMEM,
        compiler_params=SMALL,
        name="users",
    )(*pieces, *errors, users, noise)


def local(user_factors, item_factors, ratings, observed, plan, user_noise, item_noise):
    blk, shard = lax.axis_size("blk"), lax.axis_size("shard")
    ring = shard // TWINS
    user_rows = user_factors.shape[0]
    piece_rows = item_factors.shape[0]
    rows = piece_rows * TWINS
    user_rate = user_scale / ratings.shape[2]
    item_rate = item_scale / (shard * user_rows)
    strata = ratings.shape[0]
    x = lax.axis_index("shard") // TWINS
    twin = lax.axis_index("shard") % TWINS

    code, share = begin(plan, item_factors, blk)
    bits = (blk - 1).bit_length()

    def one(t, users, share):
        at = jnp.stack([t, x]).astype(jnp.int32)
        noise = lax.dynamic_slice(item_noise, (t, x * rows, 0), (1, rows, item_noise.shape[2]))[0]
        flipped = moved(share, blk)
        ready = prepare(at, observed, ratings, user_factors, users)
        flipped, ready, noise = lax.optimization_barrier((flipped, ready, noise))
        coded, users, users_half, turned = ready
        items = share + flipped
        half = items.astype(jnp.bfloat16)
        order = list(range(1, ring))
        away = {k: moved(half, 0, k) for k in order}
        drift = lax.dynamic_index_in_dim(user_noise, t, keepdims=False)
        kept = jnp.where(twin == 0, items - item_rate * prior * items + noise, 0.0)
        error, total = piece_errors(0, half, users_half, turned, coded)
        half, total, coded = lax.optimization_barrier((half, total, coded))
        pieces, errors = [half], [error]
        for k in order:
            error, grad = piece_errors(k, away[k], users_half, turned, coded)
            pieces.append(away[k])
            errors.append(error)
            total = total + moved(grad, 0, -k)
        users = users_update(pieces, errors, users, drift, user_rate)
        return users, kept + item_rate * total

    def none(t, users, share):
        mine = lax.dynamic_slice_in_dim(share, twin * piece_rows, piece_rows, 0)
        given = lax.dynamic_slice_in_dim(share, (1 - twin) * piece_rows, piece_rows, 0)
        piece = mine + moved(given, blk)
        return users, jnp.concatenate([piece, piece], 0)

    def trip(t, carry):
        users, share = carry
        step = (code >> (t * bits)) & ((1 << bits) - 1)
        return lax.cond(t < strata, one, none, t, users, rotated(share, step))

    users, items = lax.fori_loop(0, strata + 1, trip, (jnp.zeros_like(user_factors), share))
    return users, items[:piece_rows]


def solution(mesh):
    in_specs = (
        P(("blk", "shard"), None),
        P(("blk", "shard"), None),
        P(None, ("blk", "shard"), None),
        P(None, ("blk", "shard"), None),
        P(),
        P(None, ("blk", "shard"), None),
        P(None, "blk", None),
    )
    out_specs = (P(("blk", "shard"), None), P(("blk", "shard"), None))
    return jax.shard_map(local, mesh=mesh, in_specs=in_specs, out_specs=out_specs, check_vma=False)
```
